32 devices in a mesh: expert: 4 (over x, core), hidden: 8 (over z, y).
Axes of the slice: x: 2, y: 2, z: 4, core: 2. Of those that a mesh axis runs over, the one named last changes fastest.
Arguments:
- tokens: bfloat16 [128, 6144], P(('expert', 'hidden')), may hold values from -33 to 33
- norm_gain: float32 [6144], replicated, may hold values from 0.1 to 1.9
- gate_weight: bfloat16 [4, 6144, 8192], P('expert', None, 'hidden'), may hold values from -0.078125 to 0.078125
- up_weight: bfloat16 [4, 6144, 8192], P('expert', None, 'hidden'), may hold values from -0.078125 to 0.078125
- down_weight: bfloat16 [4, 8192, 6144], P('expert', 'hidden'), may hold values from -0.09375 to 0.09375
- expert_ids: int32 [128, 2], P('expert'), may hold values from 0 to 3, all different within a row; in each aligned block of 4 rows (0 to 3, 4 to 7, ...) at most 2 rows name the same one
- route_weight: float32 [128, 2], P('expert'), may hold values from 0.2 to 1
Outputs:
- settled_state: bfloat16 [128, 6144], P(('expert', 'hidden'))
The draws below stay inside these ranges and needn't reach their ends.
Inputs may be any that keep to these rules, and one draw needn't show every extreme that they name: `expert_ids`: in each aligned block of 4 rows (the tokens of one device) the two ids of a row differ and no expert is named more than 2 times; some expert is named exactly 2 times.
All inputs are finite; a program needn't handle non-finite values.
Results may differ from the reference program's by a relative error of at most 0.0085.
Values may be sent and summed in bfloat16 or wider, within the bound.
A program may use at most 64 MiB of HBM per device.

```python
import math
import jax
import jax.numpy as jnp
import numpy as np
from jax import lax

D = 6144
FF = 8192
TOK_DEV = 4
ITERS = 2
EXPERTS = 4
CAP = 2
TOKENS = 128
N_HIDDEN = 8


def draw_tokens(key, part):
    noise_key, row_key, column_key = jax.random.split(key, 3)
    row_scale = jnp.exp(jax.random.uniform(row_key, (TOKENS, 1), jnp.float32, math.log(0.25), math.log(2.5)))
    column_scale = jnp.exp(jax.random.uniform(column_key, (1, D), jnp.float32, math.log(0.25), math.log(2.5)))
    base = jnp.clip(jax.random.normal(noise_key, (TOKENS, D), jnp.float32), -4.0, 4.0)
    return (base * row_scale * column_scale).astype(jnp.bfloat16)


def spiked(result, own_key, source, target, shards_of, factor):
    owner, partner = [(jnp.arange(result.shape[axis_at]) // (result.shape[axis_at] // shards_of)).reshape([-1 if axis == axis_at else 1 for axis in range(result.ndim)]) for axis_at in (source, target)]
    chosen = jax.random.permutation(own_key, shards_of)[partner]
    strong = (owner == chosen) | (owner == (partner + shards_of // 2) % shards_of)
    return jnp.where(strong, factor * result, result)


def steps_of(rng, dims, pieces, least, high):
    def one(axis_at, blocks):
        heights = jax.random.uniform(jax.random.fold_in(jax.random.fold_in(rng, 6), axis_at), (blocks,), jnp.float32, least / len(pieces), high / len(pieces))
        return jnp.repeat(jnp.exp(heights), dims[axis_at] // blocks).reshape((-1,) + (1,) * (len(dims) - axis_at - 1))

    gain = one(*pieces[0])
    for cut in pieces[1:]:
        gain = gain * one(*cut)
    return gain


def routed_block(rng, own, number, rows, amount, top, limit, lean):
    sequence = jax.random.permutation(rng, amount)
    packed, usual = portions_of(amount, rows * top, limit, lean, True), portions_of(amount, rows * top, limit, lean, False)
    places = jnp.arange(amount)

    def named(tallies, turn):
        used = int((tallies > 0).sum())
        fixed = max(1, used // 4)
        shifted = fixed + (places - fixed + turn * (used - fixed)) % max(1, amount - fixed)
        return jnp.zeros((amount,), jnp.int32).at[sequence[jnp.where(places < fixed, places, shifted)]].set(jnp.asarray(tallies, jnp.int32))

    tallies = jnp.where(number % 4 == 0, named(packed, number // 4), named(usual, number - number // 4 - 1))
    mixed = jax.random.permutation(jax.random.fold_in(own, 3), amount)
    donor, receiver = mixed[0:amount // 2 * 2:2], mixed[1:amount // 2 * 2:2]
    room = jnp.minimum(tallies[donor] - 1, limit - tallies[receiver]) // 2
    room = jnp.where((donor == sequence[0]) | (receiver == sequence[0]) | (tallies[receiver] == 0), 0, jnp.maximum(room, 0))
    shifted = jax.random.randint(jax.random.fold_in(own, 4), (amount // 2,), 0, 1 << 20) % (room + 1)
    tallies = tallies.at[donor].add(-shifted).at[receiver].add(shifted)
    members = jnp.searchsorted(jnp.cumsum(tallies), jnp.arange(rows * top), side="right").astype(jnp.int32)
    table = members.reshape(top, rows).T
    table = table[jax.random.permutation(jax.random.fold_in(own, 1), rows)]
    turn = jax.random.randint(jax.random.fold_in(own, 2), (rows, 1), 0, top)
    return jnp.take_along_axis(table, (jnp.arange(top)[None, :] + turn) % top, axis=1)


def portions_of(amount, total, most, slope, full):
    portions = [(1 << 20) // math.isqrt(rank ** slope) + 1 for rank in range(1, amount + 1)]
    largest = most if full else min(most, max(-(-total // amount), total * portions[0] // sum(portions)))
    least = 1 if total - largest >= amount - 1 else 0
    holding, rest = [largest] + [least] * (amount - 1), total - largest - least * (amount - 1)
    while rest > 0:
        candidates = [i for i in range(1, amount) if holding[i] < largest] or [i for i in range(1, amount) if holding[i] < most]
        whole, budget = sum([portions[i] for i in candidates]), rest
        for i in candidates:
            more = min(most - holding[i], max(1, budget * portions[i] // whole), rest)
            holding[i] = holding[i] + more
            rest = rest - more
    return np.array(holding)


def scatter_about(key, extent, deviation, bound, cuts=(), held_as=jnp.bfloat16):
    entries = deviation * jax.random.normal(key, extent, jnp.float32)
    if cuts:
        entries = entries * steps_of(key, extent, cuts, -0.22, 0.18)
    return jnp.clip(entries, -bound, bound).astype(held_as)


def bell_draw_with(stream_key, shape, deviation, limit, shards, heavy, held_as=jnp.bfloat16):
    entries = deviation * jax.random.normal(stream_key, shape, jnp.float32)
    if shards:
        entries = entries * steps_of(stream_key, shape, shards, -0.22, 0.18)
    return jnp.clip(spiked(entries, jax.random.fold_in(stream_key, 3), *heavy), -limit, limit).astype(held_as)


def setup_inputs(seed: int = 0) -> dict:
    seeds = jax.random.split(jax.random.key(seed), 8)
    tokens = draw_tokens(jax.random.fold_in(seeds[7], 71), 0)
    norm_gain = jnp.clip(1.0 + 0.18 * jax.random.normal(seeds[1], (D,), jnp.float32), 0.1, 1.9)
    gate_weight = scatter_about(seeds[2], (EXPERTS, D, FF), D ** -0.5, 0.078125, ((0, 4), (2, 8)))
    up_weight = scatter_about(seeds[3], (EXPERTS, D, FF), D ** -0.5, 0.078125, ((0, 4), (2, 8)))
    down_weight = bell_draw_with(seeds[4], (EXPERTS, FF, D), FF ** -0.5, 0.09375, ((0, 4), (1, 8)), (1, 2, 8, 2.0))
    expert_ids_keys = jax.random.split(jax.random.fold_in(seeds[5], 1), TOKENS // TOK_DEV)
    expert_ids_turns = jax.random.permutation(jax.random.fold_in(seeds[5], 3), TOKENS // TOK_DEV)
    expert_ids = jax.vmap(lambda own, number: routed_block(jax.random.fold_in(seeds[5], 2), own, number, TOK_DEV, EXPERTS, 2, CAP, 2))(expert_ids_keys, expert_ids_turns).reshape((TOKENS, 2))
    route_weight = jnp.clip(0.2 + 0.8 * jax.random.uniform(seeds[6], (TOKENS, 2), jnp.float32) ** steps_of(seeds[6], (TOKENS, 2), ((0, 4),), -0.2, 0.2), 0.2, 1.0)
    return dict(tokens=tokens, norm_gain=norm_gain, gate_weight=gate_weight, up_weight=up_weight, down_weight=down_weight, expert_ids=expert_ids, route_weight=route_weight)


EPSILON = 1e-05
NUDGE = 0.5

def rms_norm(values, norm_gain):
    widened = values.astype(jnp.float32)
    mean_square = lax.optimization_barrier(jnp.mean(widened * widened, axis=-1, keepdims=True))
    return (widened * lax.rsqrt(mean_square + EPSILON) * norm_gain).astype(jnp.bfloat16)

def expert_outputs(normed, gate_panel, up_panel, down_panel, chosen):
    inputs = jnp.take(normed, chosen, axis=0)
    gate_value = jnp.dot(inputs, gate_panel, preferred_element_type=jnp.float32)
    up_value = jnp.dot(inputs, up_panel, preferred_element_type=jnp.float32)
    hidden_units = (jax.nn.silu(gate_value) * up_value).astype(jnp.bfloat16)
    unit_block = FF // N_HIDDEN

    def add_block(block_index, total):
        start = (block_index * unit_block).astype(jnp.int32)
        units = lax.dynamic_slice_in_dim(hidden_units, start, unit_block, 1)
        panel = lax.dynamic_slice_in_dim(down_panel, start, unit_block, 0)
        partial_sum = jnp.dot(units, panel, preferred_element_type=jnp.float32).astype(jnp.bfloat16)
        partial_sum = lax.optimization_barrier(partial_sum)
        return total + partial_sum.astype(jnp.float32)
    total = lax.fori_loop(0, N_HIDDEN, add_block, jnp.zeros((chosen.shape[0], D), jnp.float32))
    return total.astype(jnp.bfloat16)

def reference(tokens, norm_gain, gate_weight, up_weight, down_weight, expert_ids, route_weight):
    state = tokens
    token_index = jnp.arange(TOKENS, dtype=jnp.int32)
    for iteration in range(ITERS):
        normed = rms_norm(state, norm_gain)

        def one_expert(expert):
            routed = jnp.any(expert_ids == expert, axis=1)
            order_keys = jnp.where(routed, 0, 1).astype(jnp.int32)
            chosen = jnp.argsort(order_keys, stable=True)[:TOKENS // 2].astype(jnp.int32)
            values = expert_outputs(normed, gate_weight[expert], up_weight[expert], down_weight[expert], chosen)
            return jnp.zeros((TOKENS, D), jnp.bfloat16).at[chosen].set(values)
        outputs = lax.map(one_expert, jnp.arange(EXPERTS, dtype=jnp.int32))
        first = outputs[expert_ids[:, 0], token_index].astype(jnp.float32) * route_weight[:, 0:1]
        second = outputs[expert_ids[:, 1], token_index].astype(jnp.float32) * route_weight[:, 1:2]
        mixed = first + second
        state = (NUDGE * state.astype(jnp.float32) + NUDGE * (tokens.astype(jnp.float32) + mixed)).astype(jnp.bfloat16)
    return state
```

```python
import functools
import math

import jax
import jax.numpy as jnp
from jax import lax
from jax.experimental import pallas as pl
from jax.experimental.pallas import tpu as pltpu
from jax.sharding import PartitionSpec as P

ITERS = 2
EPSILON = 1e-05
NUDGE = 0.5
CHUNKS = 4
LANES = 128
MESH = pl.DeviceIdType.MESH
f32, bf16 = jnp.float32, jnp.bfloat16


class Plan:
    def __init__(self, experts, hidden, tok, width, units):
        self.E, self.H, self.tok, self.D, self.U = experts, hidden, tok, width, units
        self.C = 2
        self.X = experts // self.C
        self.Y = 2
        self.Z = hidden // self.Y
        self.R = self.Z * tok
        self.NB = self.C * self.X * self.Y
        self.K = width // CHUNKS
        self.rows = self.NB * self.R
        self.numbers = {}

    def number(self, key):
        return self.numbers.setdefault(key, len(self.numbers))

    def block(self, rc, rx, ry):
        return (rc * self.X + rx) * self.Y + ry


def all_keys(p):
    for rc in range(p.C):
        for rx in range(p.X):
            if rc or rx:
                p.number(("route", rc, rx))
    for i in range(CHUNKS):
        for d in range(1, p.Z):
            p.number(("z", i, d))
        for b in range(1, p.NB):
            p.number(("blk", i, b))
        p.number(("core", i))
        f, s = (p.X, p.Y) if i % 2 == 0 else (p.Y, p.X)
        for d in range(1, f):
            p.number(("first", i, d))
        for d in range(1, s):
            p.number(("second", i, d))
        for d in range(1, p.Z):
            p.number(("back", i, d))


def tiles(count, body):
    if count == 1:
        body(0)
    else:
        pl.loop(0, count)(body)


def compact_kernel(p, tokens_ref, gain_ref, route_ref, gate_hbm, up_hbm, down_hbm, out_ref,
           wg, wu, wd, xg, n4, z1, asm, acc, hid, route_in, wrow, state, keep, cs, cr,
           fs, fr, held, ss, sr, usum, own, bs, br, wsem, send_sem, recv_sem):
    C, X, Y, Z, R, K, T = p.C, p.X, p.Y, p.Z, p.R, p.K, p.tok
    e, h = lax.axis_index("expert"), lax.axis_index("hidden")
    x, c = e // C, e % C
    z, y = h // Y, h % Y

    def at(rc=0, rx=0, ry=0, rz=0):
        return ((x + rx) % X * C + (c + rc) % C, (z + rz) % Z * Y + (y + ry) % Y)

    loads = []
    for i in range(CHUNKS):
        rows = pl.ds(i * K, K)
        loads.append(pltpu.make_async_copy(gate_hbm.at[0, rows, :], wg.at[rows, :], wsem.at[3 * i]))
        loads.append(pltpu.make_async_copy(up_hbm.at[0, rows, :], wu.at[rows, :], wsem.at[3 * i + 1]))
    for i in range(CHUNKS):
        cols = pl.ds(i * K, K)
        loads.append(pltpu.make_async_copy(down_hbm.at[0, :, cols], wd.at[i], wsem.at[3 * i + 2]))
    for load in loads:
        load.start()

    barrier = pltpu.get_barrier_semaphore()
    partners = [at(rc=rc, rx=rx) for rc in range(C) for rx in range(X) if rc or rx]
    partners += [at(ry=d) for d in range(1, Y)] + [at(rz=d) for d in range(1, Z)]
    for partner in partners:
        pl.semaphore_signal(barrier, inc=1, device_id=partner, device_id_type=MESH)

    state[...] = tokens_ref[...].astype(f32)
    pl.semaphore_wait(barrier, len(partners))

    def copy(key, src, dst, to):
        n = p.number(key)
        return pltpu.make_async_remote_copy(
            src_ref=src, dst_ref=dst, send_sem=send_sem.at[n], recv_sem=recv_sem.at[n],
            device_id=to, device_id_type=MESH)

    def send(sent, *args):
        made = copy(*args)
        made.start()
        sent.append(made)

    def arrived(key, dst):
        copy(key, dst, dst, at(rc=1)).wait_recv()

    routes = []
    for rc in range(C):
        for rx in range(X):
            if rc or rx:
                send(routes, ("route", (-rc) % C, (-rx) % X), route_ref,
                     route_in.at[((-rc) % C) * X + (-rx) % X], at(rc=rc, rx=rx))

    def iteration(it, _):
        first_time = it == 0

        values = state[...]
        mean_square = jnp.sum(values * values, axis=-1, keepdims=True) / p.D
        normed = (values * lax.rsqrt(mean_square + EPSILON) * gain_ref[...]).astype(bf16)
        for i in range(CHUNKS):
            n4[i] = normed[:, i * K:(i + 1) * K]
        sent = []
        for i in range(CHUNKS):
            for d in range(1, Z):
                send(sent, ("z", i, Z - d), n4.at[i], z1.at[i, Z - d], at(rz=d))

        def block_to(i, b_from, rc, rx, ry):
            b, rest = b_from % Y, b_from // Y
            fx, fc = rest % X, rest // X
            there = p.block((fc - rc) % C, (fx - rx) % X, (b - ry) % Y)
            send(sent, ("blk", i, there), xg.at[i, b_from], xg.at[i, there], at(rc, rx, ry))

        def got(i, b):
            arrived(("blk", i, b), xg.at[i, b])

        def level1(i):
            for d in range(1, Z):
                arrived(("z", i, d), z1.at[i, d])
            asm[0:T, :] = n4[i].astype(f32)
            for d in range(1, Z):
                asm[d * T:(d + 1) * T, :] = z1[i, d].astype(f32)
            xg[i, 0] = asm[...].astype(bf16)
            for d in range(1, Y):
                block_to(i, 0, 0, 0, d)
            for d in range(1, X):
                block_to(i, 0, 0, d, 0)
            block_to(i, 0, 1, 0, 0)

        def level2(i):
            if i % 2 == 0:
                for ry in range(1, Y):
                    b = p.block(0, 0, ry)
                    got(i, b)
                    for d in range(1, X):
                        block_to(i, b, 0, d, 0)
                    block_to(i, b, 1, 0, 0)
                for rx in range(1, X):
                    b = p.block(0, rx, 0)
                    got(i, b)
                    block_to(i, b, 1, 0, 0)
            else:
                for rx in range(1, X):
                    b = p.block(0, rx, 0)
                    got(i, b)
                    for d in range(1, Y):
                        block_to(i, b, 0, 0, d)
                    block_to(i, b, 1, 0, 0)
                for ry in range(1, Y):
                    b = p.block(0, 0, ry)
                    got(i, b)
                    block_to(i, b, 1, 0, 0)

        def level3(i):
            for rx in range(1, X):
                for ry in range(1, Y):
                    b = p.block(0, rx, ry)
                    got(i, b)
                    block_to(i, b, 1, 0, 0)

        per = max(1, min(p.NB, 128 // R))
        row_tiles = p.NB // per
        high = per * R
        wide = min(512, p.U)

        def multiply(i):
            for b in range(X * Y, p.NB):
                got(i, b)

            @pl.when(first_time)
            def _():
                loads[2 * i].wait()
                loads[2 * i + 1].wait()

            def column(n):
                cols = pl.ds(pl.multiple_of(n * wide, wide), wide)

                def row(m):
                    block = xg[i, pl.ds(m * per, per)].reshape(high, K)
                    place = pl.ds(pl.multiple_of(m * high, high), high)
                    for side, weight in ((0, wg), (1, wu)):
                        product = jnp.dot(block, weight[pl.ds(i * K, K), cols], preferred_element_type=f32)
                        if i == 0:
                            acc[side, place, cols] = product
                        else:
                            acc[side, place, cols] += product

                tiles(row_tiles, row)

            tiles(p.U // wide, column)

        for t in range(CHUNKS + 3):
            if t < CHUNKS:
                level1(t)
            if 0 <= t - 1 < CHUNKS:
                level2(t - 1)
            if 0 <= t - 2 < CHUNKS:
                level3(t - 2)
            if 0 <= t - 3 < CHUNKS:
                multiply(t - 3)
        for made in sent:
            made.wait_send()

        @pl.when(first_time)
        def _():
            lane = lax.broadcasted_iota(jnp.int32, (T, LANES), 1)
            for rc in range(C):
                for rx in range(X):
                    if rc or rx:
                        arrived(("route", rc, rx), route_in.at[rc * X + rx])
                    for ry in range(Y):
                        for rz in range(Z):
                            _, whose = at(ry=ry, rz=rz)
                            if rc or rx:
                                part = route_in[rc * X + rx, whose]
                            else:
                                part = route_ref[whose]
                            mine = jnp.sum(jnp.where(lane == e, part, 0.0), axis=1, keepdims=True)
                            base = p.block(rc, rx, ry) * R + rz * T
                            wrow[base:base + T, :] = jnp.broadcast_to(mine, (T, LANES))

        def activate(n):
            cols = pl.ds(pl.multiple_of(n * LANES, LANES), LANES)

            def row(m):
                place = pl.ds(pl.multiple_of(m * high, high), high)
                gate = acc[0, place, cols]
                units = gate / (1.0 + jnp.exp(-gate)) * acc[1, place, cols]
                hid[place, cols] = (units * wrow[place, :]).astype(bf16)

            tiles(row_tiles, row)

        tiles(p.U // LANES, activate)

        sent = []
        half = p.rows // C
        narrow = 512 if K % 512 == 0 else LANES

        def down(i):
            @pl.when(first_time)
            def _():
                loads[2 * CHUNKS + i].wait()

            def column(n):
                cols = pl.ds(pl.multiple_of(n * narrow, narrow), narrow)

                def row(m):
                    place = pl.ds(pl.multiple_of(m * 64, 64), 64)
                    other = pl.ds(pl.multiple_of(half + m * 64, 64), 64)
                    cs[i, place, cols] = jnp.dot(hid[other, :], wd[i, :, cols], preferred_element_type=f32).astype(bf16)
                    keep[i % 2, place, cols] = jnp.dot(hid[place, :], wd[i, :, cols], preferred_element_type=f32)

                tiles(half // 64, row)

            tiles(K // narrow, column)
            send(sent, ("core", i), cs.at[i], cr.at[i], at(rc=1))

        def dims(i):
            if i % 2 == 0:
                return X, Y, lambda a, b: a * Y + b, lambda d: at(rx=d), lambda d: at(ry=d)
            return Y, X, lambda a, b: b * Y + a, lambda d: at(ry=d), lambda d: at(rx=d)

        def reduce1(i):
            arrived(("core", i), cr.at[i])
            F, S, place, to_first, _ = dims(i)
            for a in list(range(1, F)) + [0]:
                for b in range(S):
                    rows = pl.ds(place(a, b) * R, R)
                    total = keep[i % 2, rows, :] + cr[i, rows, :].astype(f32)
                    if a:
                        fs[i, (a - 1) * S + b] = total.astype(bf16)
                    else:
                        held[i % 2, b] = total
                if a:
                    send(sent, ("first", i, a), fs.at[i, pl.ds((a - 1) * S, S)],
                         fr.at[i, pl.ds((a - 1) * S, S)], to_first(a))

        def reduce2(i):
            F, S, _, _, to_second = dims(i)
            for a in range(1, F):
                arrived(("first", i, a), fr.at[i, pl.ds((a - 1) * S, S)])
            for b in list(range(1, S)) + [0]:
                total = held[i % 2, b]
                for a in range(1, F):
                    total = total + fr[i, (a - 1) * S + b].astype(f32)
                if b:
                    ss[i, b - 1] = total.astype(bf16)
                    send(sent, ("second", i, b), ss.at[i, b - 1], sr.at[i, b - 1], to_second(b))
                else:
                    usum[i % 2] = total

        def reduce3(i):
            S = dims(i)[1]
            total = usum[i % 2]
            for b in range(1, S):
                arrived(("second", i, b), sr.at[i, b - 1])
                total = total + sr[i, b - 1].astype(f32)
            asm[...] = total
            for d in range(1, Z):
                bs[i, d - 1] = asm[d * T:(d + 1) * T, :].astype(bf16)
                send(sent, ("back", i, d), bs.at[i, d - 1], br.at[i, d - 1], at(rz=d))
            own[i] = asm[0:T, :]

        def settle(i):
            mixed = own[i]
            for d in range(1, Z):
                arrived(("back", i, d), br.at[i, d - 1])
                mixed = mixed + br[i, d - 1].astype(f32)
            cols = pl.ds(i * K, K)
            fresh = (NUDGE * state[:, cols] + NUDGE * (tokens_ref[:, cols].astype(f32) + mixed)).astype(bf16)
            state[:, cols] = fresh.astype(f32)
            out_ref[:, cols] = fresh

        steps = (down, reduce1, reduce2, reduce3, settle)
        for t in range(CHUNKS + len(steps) - 1):
            for lag, step in enumerate(steps):
                if 0 <= t - lag < CHUNKS:
                    step(t - lag)
        for made in sent:
            made.wait_send()
        return 0

    lax.fori_loop(0, ITERS, iteration, 0)
    for made in routes:
        made.wait_send()


def on_device_compact(experts, hidden, tokens, norm_gain, gate_weight, up_weight, down_weight, expert_ids, route_weight):
    tok, width = tokens.shape
    p = Plan(experts, hidden, tok, width, gate_weight.shape[2])
    all_keys(p)
    lanes = jnp.arange(LANES, dtype=jnp.int32)[None, :]
    table = (jnp.where(expert_ids[:, 0:1] == lanes, route_weight[:, 0:1], 0.0)
             + jnp.where(expert_ids[:, 1:2] == lanes, route_weight[:, 1:2], 0.0))
    table = table.reshape(hidden, tok, LANES)
    n, K, R, U = len(p.numbers), p.K, p.R, p.U
    S, FS = max(p.X, p.Y), max((p.X - 1) * p.Y, (p.Y - 1) * p.X)
    half = p.rows // p.C
    vmem = pltpu.VMEM
    scratch = [
        vmem((width, U), bf16), vmem((width, U), bf16), vmem((CHUNKS, U, K), bf16),
        vmem((CHUNKS, p.NB, R, K), bf16),
        vmem((CHUNKS, tok, K), bf16), vmem((CHUNKS, p.Z, tok, K), bf16), vmem((R, K), f32),
        vmem((2, p.rows, U), f32), vmem((p.rows, U), bf16),
        vmem((experts, hidden, tok, LANES), f32), vmem((p.rows, LANES), f32),
        vmem((tok, width), f32),
        vmem((2, half, K), f32), vmem((CHUNKS, half, K), bf16), vmem((CHUNKS, half, K), bf16),
        vmem((CHUNKS, FS, R, K), bf16), vmem((CHUNKS, FS, R, K), bf16),
        vmem((2, S, R, K), f32),
        vmem((CHUNKS, S - 1, R, K), bf16), vmem((CHUNKS, S - 1, R, K), bf16),
        vmem((2, R, K), f32),
        vmem((CHUNKS, tok, K), f32),
        vmem((CHUNKS, p.Z - 1, tok, K), bf16), vmem((CHUNKS, p.Z - 1, tok, K), bf16),
        pltpu.SemaphoreType.DMA((3 * CHUNKS,)),
        pltpu.SemaphoreType.DMA((n,)), pltpu.SemaphoreType.DMA((n,)),
    ]
    inside = pl.BlockSpec(memory_space=pltpu.VMEM)
    outside = pl.BlockSpec(memory_space=pl.ANY)
    return pl.pallas_call(
        functools.partial(compact_kernel, p),
        out_shape=jax.ShapeDtypeStruct((tok, width), bf16),
        in_specs=[inside] * 3 + [outside] * 3,
        out_specs=inside,
        scratch_shapes=scratch,
        compiler_params=pltpu.CompilerParams(
            collective_id=0, has_side_effects=True, vmem_limit_bytes=67_000_000),
        name="settle",
    )(tokens, norm_gain.reshape(1, width), table, gate_weight, up_weight, down_weight)


WIDE = 1024
VMEM_BYTES = 67_000_000
LINK = 46.0e3
LATENCY = {"x": 1.7, "y": 1.7, "z": 2.6, "c": 0.95}
COST = {"level1": 0.12, "level2": 0.03, "level3": 0.03, "multiply": 0.62, "activate": 0.4, "down": 0.36,
        "reduce1": 0.12, "reduce2": 0.1, "reduce3": 0.12, "settle": 0.12, "enter": 0.02, "weights": 0.3}
HEAVY = ("multiply", "down", "activate", "weights")


class Deep:
    def __init__(self, experts, hidden, tok, width, units):
        self.E, self.H, self.tok, self.D, self.U = experts, hidden, tok, width, units
        self.C, self.Y = 2, 2
        self.X, self.Z = experts // self.C, hidden // self.Y
        self.R = self.Z * tok
        self.B = self.X * self.Y
        self.NB = self.C * self.B
        self.w = WIDE if width % WIDE == 0 else LANES
        self.n = width // self.w
        self.rows = self.NB * self.R
        self.half = self.rows // self.C
        self.numbers = {}

    def number(self, key):
        return self.numbers.setdefault(key, len(self.numbers))

    def block(self, rc, rx, ry):
        return (rc * self.X + rx) * self.Y + ry

    def dims(self, i):
        if i % 2 == 0:
            return "x", "y", self.X, self.Y
        return "y", "x", self.Y, self.X

    def place(self, axis, d):
        return (0, d, 0, 0) if axis == "x" else (0, 0, d, 0)

    def take(self, i):
        return self.w + LANES if i == self.n - 1 else self.w


def orders(p):
    X, Y, Z, R, T, n, w = p.X, p.Y, p.Z, p.R, p.tok, p.n, p.w
    tasks = {}

    def z_sends(it, i):
        return [(("z", it, i, d), "z", T * p.take(i) * 2) for d in range(1, Z)]

    def core(it, i, b):
        return [(("blk", it, i, b + p.B), "c", R * p.take(i) * 2)]

    def add(name, deps=(), needs=(), sends=()):
        tasks[name] = (list(deps), list(needs), list(sends))

    for it in range(ITERS):
        for i in range(n):
            size = R * p.take(i) * 2
            first, second, F, S = p.dims(i)
            if it == 0:
                add(("enter", it, i), sends=z_sends(it, i))
                before = [("enter", it, i)]
            else:
                before = [("settle", it - 1, i)]
            sends = []
            for axis, count in ((first, F), (second, S)):
                sends += [(("blk", it, i, p.block(*p.place(axis, d)[:3])), axis, size) for d in range(1, count)]
            add(("level1", it, i), before, [("z", it, i, d) for d in range(1, Z)], sends + core(it, i, 0))
            for d in range(1, F):
                b = p.block(*p.place(first, d)[:3])
                more = []
                for g in range(1, S):
                    both = [sum(v) for v in zip(p.place(first, d), p.place(second, g))]
                    more.append((("blk", it, i, p.block(*both[:3])), second, size))
                add(("level2", it, i, d), [("level1", it, i)], [("blk", it, i, b)], more + core(it, i, b))
                for g in range(1, S):
                    both = [sum(v) for v in zip(p.place(first, d), p.place(second, g))]
                    b = p.block(*both[:3])
                    add(("level3", it, i, 0, d, g), [("level1", it, i)], [("blk", it, i, b)], core(it, i, b))
            for g in range(1, S):
                b = p.block(*p.place(second, g)[:3])
                add(("level3", it, i, 1, g, 0), [("level1", it, i)], [("blk", it, i, b)], core(it, i, b))
            local = [t for t in tasks if t[0] in ("level1", "level2", "level3") and t[1:3] == (it, i)]
            if i:
                local.append(("multiply", it, i - 1))
            if it == 0 and i == 1:
                local.append(("weights", 0, 0))
            add(("multiply", it, i), local, [("blk", it, i, b + p.B) for b in range(p.B)])
            add(("down", it, i), [("activate", it, 0)] + ([("down", it, i - 1)] if i else []), (),
                [(("core", it, i), "c", p.half * w * 2)])
            add(("reduce1", it, i), [("down", it, i)], [("core", it, i)],
                [(("first", it, i, a), first, S * R * w * 2) for a in range(1, F)])
            add(("reduce2", it, i), [("reduce1", it, i)], [("first", it, i, a) for a in range(1, F)],
                [(("second", it, i, b), second, R * w * 2) for b in range(1, S)])
            add(("reduce3", it, i), [("reduce2", it, i)], [("second", it, i, b) for b in range(1, S)],
                [(("back", it, i, d), "z", T * w * 2) for d in range(1, Z)])
            add(("settle", it, i), [("reduce3", it, i)] + ([("settle", it, i - 1)] if i else []),
                [("back", it, i, d) for d in range(1, Z)], z_sends(it + 1, i) if it + 1 < ITERS else [])
        add(("activate", it, 0), [("multiply", it, n - 1), ("weights", 0, 0)])
    add(("weights", 0, 0), (), [("route", r) for r in range(1, p.C * X)])

    for _, _, sends in tasks.values():
        for key, _, _ in sends:
            p.number(key)
    for r in range(1, p.C * X):
        p.number(("route", r))

    rate = {"x": LINK, "y": LINK, "z": LINK * 3 / Z, "c": 600.0e3}
    free = dict.fromkeys(rate, 0.0)
    arrival = {("route", r): 3.0 for r in range(1, p.C * X)}
    now, order, left = 0.0, [], dict(tasks)
    done = set()
    while left:
        best = None
        for position, (name, (deps, needs, _)) in enumerate(left.items()):
            if any(d not in done for d in deps) or any(k not in arrival for k in needs):
                continue
            ready = max([now] + [arrival[k] for k in needs])
            rank = (ready, name[0] in HEAVY, position)
            if best is None or rank < best[0]:
                best = (rank, name)
        (ready, _, _), name = best
        now = ready + COST[name[0]]
        for key, link, size in left[name][2]:
            begin = max(free[link], now)
            free[link] = begin + size / rate[link]
            arrival[key] = free[link] + LATENCY[link]
        done.add(name)
        order.append(name)
        del left[name]
    return order, now


def kernel(p, order, tokens_ref, gain_ref, ids_ref, weight_ref, gate_hbm, up_hbm, down_hbm, out_ref,
           wg, wu, wd, xg, n4, z1, asm, acc, hid, tab, tabs, wrow, state, keep, cs, cr,
           fs, fr, held, ss, sr, usum, own, bs, br, wsem, send_sem, recv_sem):
    C, X, Y, Z, R, w, T, n = p.C, p.X, p.Y, p.Z, p.R, p.w, p.tok, p.n
    e, h = lax.axis_index("expert"), lax.axis_index("hidden")
    x, c = e // C, e % C
    z, y = h // Y, h % Y

    def at(rc=0, rx=0, ry=0, rz=0):
        return ((x + rx) % X * C + (c + rc) % C, (z + rz) % Z * Y + (y + ry) % Y)

    loads = []
    for i in range(n):
        rows = pl.ds(i * w, w)
        loads.append(pltpu.make_async_copy(gate_hbm.at[0, rows, :], wg.at[rows, :], wsem.at[3 * i]))
        loads.append(pltpu.make_async_copy(up_hbm.at[0, rows, :], wu.at[rows, :], wsem.at[3 * i + 1]))
    for i in range(n):
        loads.append(pltpu.make_async_copy(down_hbm.at[0, :, pl.ds(i * w, w)], wd.at[i], wsem.at[3 * i + 2]))

    barrier = pltpu.get_barrier_semaphore()
    partners = [at(rc=rc, rx=rx) for rc in range(C) for rx in range(X) if rc or rx]
    partners += [at(ry=d) for d in range(1, Y)] + [at(rz=d) for d in range(1, Z)]
    for partner in partners:
        pl.semaphore_signal(barrier, inc=1, device_id=partner, device_id_type=MESH)
    for load in loads:
        load.start()

    sent = []

    def copy(key, src, dst, to):
        k = p.numbers[key]
        return pltpu.make_async_remote_copy(
            src_ref=src, dst_ref=dst, send_sem=send_sem.at[k], recv_sem=recv_sem.at[k],
            device_id=to, device_id_type=MESH)

    def send(*args):
        made = copy(*args)
        made.start()
        sent.append(made)

    def arrived(key, dst):
        copy(key, dst, dst, at(rc=1)).wait_recv()

    def scales(square):
        scale = lax.rsqrt(square / p.D + EPSILON)
        high = scale.astype(bf16).astype(f32)
        middle = (scale - high).astype(bf16).astype(f32)
        low = scale - high - middle
        lane = lax.broadcasted_iota(jnp.int32, (T, LANES), 1)
        parts = jnp.where(lane == 0, high, jnp.where(lane == 1, middle, jnp.where(lane == 2, low, 0.0)))
        return parts.astype(bf16)

    squares = [None] * ITERS

    def prepare(it, i, values):
        cols = pl.ds(i * w, w)
        square = jnp.sum(values * values, axis=-1, keepdims=True)
        squares[it] = square if i == 0 else squares[it] + square
        n4[it, i, :, 0:w] = (values * gain_ref[:, cols]).astype(bf16)
        if i == n - 1:
            n4[it, i, :, w:w + LANES] = scales(squares[it])

    def enter(it, i):
        for d in range(1, Z):
            send(("z", it, i, Z - d), n4.at[it, i, :, pl.ds(0, p.take(i))],
                 z1.at[it, i, Z - d, :, pl.ds(0, p.take(i))], at(rz=d))

    values = tokens_ref[...].astype(f32)
    state[...] = values
    for i in range(n):
        prepare(0, i, values[:, i * w:(i + 1) * w])
    L = p.H * T
    which = lax.broadcasted_iota(jnp.int32, (p.E, L), 0)
    tab[...] = jnp.zeros_like(tab)
    tab[:, 0:L] = (jnp.where(ids_ref[0:1, :] == which, weight_ref[0:1, :], 0.0)
                   + jnp.where(ids_ref[1:2, :] == which, weight_ref[1:2, :], 0.0))
    pl.semaphore_wait(barrier, len(partners))

    def weights(*_):
        lane = lax.broadcasted_iota(jnp.int32, (T, LANES), 1)
        token = lax.broadcasted_iota(jnp.int32, (T, LANES), 0)
        expert = lax.broadcasted_iota(jnp.int32, (p.E, LANES), 0)
        for rc in range(C):
            for rx in range(X):
                r = rc * X + rx
                if r:
                    arrived(("route", r), tabs.at[r])
                table = tabs[r] if r else tab[...]
                mine = jnp.sum(jnp.where(expert == e, table, 0.0), axis=0, keepdims=True)
                for ry in range(Y):
                    for rz in range(Z):
                        _, whose = at(ry=ry, rz=rz)
                        part = jnp.where(lane == whose * T + token, mine, 0.0)
                        base = p.block(rc, rx, ry) * R + rz * T
                        wrow[base:base + T, :] = jnp.broadcast_to(
                            jnp.sum(part, axis=1, keepdims=True), (T, LANES))

    def piece(it, i, b):
        return xg.at[it, i, b, :, pl.ds(0, p.take(i))]

    def block_to(it, i, b_from, rc, rx, ry):
        b, rest = b_from % Y, b_from // Y
        fx, fc = rest % X, rest // X
        there = p.block((fc - rc) % C, (fx - rx) % X, (b - ry) % Y)
        send(("blk", it, i, there), piece(it, i, b_from), piece(it, i, there), at(rc, rx, ry))

    def got(it, i, b):
        arrived(("blk", it, i, b), piece(it, i, b))

    def level1(it, i):
        wide = p.take(i)
        for d in range(1, Z):
            arrived(("z", it, i, d), z1.at[it, i, d, :, pl.ds(0, wide)])
        asm[0:T, 0:wide] = n4[it, i, :, 0:wide].astype(f32)
        for d in range(1, Z):
            asm[d * T:(d + 1) * T, 0:wide] = z1[it, i, d, :, 0:wide].astype(f32)
        xg[it, i, 0, :, 0:wide] = asm[:, 0:wide].astype(bf16)
        first, second, F, S = p.dims(i)
        for axis, count in ((first, F), (second, S)):
            for d in range(1, count):
                block_to(it, i, 0, *p.place(axis, d)[:3])
        block_to(it, i, 0, 1, 0, 0)

    def level2(it, i, d):
        first, second, _, S = p.dims(i)
        b = p.block(*p.place(first, d)[:3])
        got(it, i, b)
        for g in range(1, S):
            block_to(it, i, b, *p.place(second, g)[:3])
        block_to(it, i, b, 1, 0, 0)

    def level3(it, i, kind, d, g):
        first, second, _, _ = p.dims(i)
        if kind:
            b = p.block(*p.place(second, d)[:3])
        else:
            b = p.block(*[sum(v) for v in zip(p.place(first, d), p.place(second, g))][:3])
        got(it, i, b)
        block_to(it, i, b, 1, 0, 0)

    def multiply(it, i):
        for b in range(p.B, p.NB):
            got(it, i, b)
        if it == 0:
            loads[2 * i].wait()
            loads[2 * i + 1].wait()
        block = xg[it, i, :, :, 0:w].reshape(p.rows, w)
        for side, weight in ((0, wg), (1, wu)):
            product = jnp.dot(block, weight[i * w:(i + 1) * w, :], preferred_element_type=f32)
            if i == 0:
                acc[side] = product
            else:
                acc[side] += product

    def activate(it, _):
        parts = xg[it, n - 1, :, :, w:w + LANES].reshape(p.rows, LANES).astype(f32)
        scale = jnp.broadcast_to(jnp.sum(parts, axis=1, keepdims=True), (p.rows, LANES))
        mine = wrow[...]
        for k in range(p.U // LANES):
            cols = slice(k * LANES, (k + 1) * LANES)
            gate = acc[0, :, cols] * scale
            units = gate / (1.0 + jnp.exp(-gate)) * (acc[1, :, cols] * scale)
            hid[:, cols] = (units * mine).astype(bf16)

    def down(it, i):
        if it == 0:
            loads[2 * n + i].wait()
        product = jnp.dot(hid[...], wd[i], preferred_element_type=f32)
        cs[it, i] = product[p.half:, :].astype(bf16)
        send(("core", it, i), cs.at[it, i], cr.at[it, i], at(rc=1))
        keep[i] = product[:p.half, :]

    def reduce1(it, i):
        arrived(("core", it, i), cr.at[it, i])
        first, _, F, S = p.dims(i)
        for a in list(range(1, F)) + [0]:
            for b in range(S):
                b_at = p.block(0, a, b) if first == "x" else p.block(0, b, a)
                rows = pl.ds(b_at * R, R)
                total = keep[i, rows, :] + cr[it, i, rows, :].astype(f32)
                if a:
                    fs[it, i, (a - 1) * S + b] = total.astype(bf16)
                else:
                    held[i, b] = total
            if a:
                send(("first", it, i, a), fs.at[it, i, pl.ds((a - 1) * S, S)],
                     fr.at[it, i, pl.ds((a - 1) * S, S)], at(*p.place(first, a)[:3]))

    def reduce2(it, i):
        _, second, F, S = p.dims(i)
        for a in range(1, F):
            arrived(("first", it, i, a), fr.at[it, i, pl.ds((a - 1) * S, S)])
        for b in list(range(1, S)) + [0]:
            total = held[i, b]
            for a in range(1, F):
                total = total + fr[it, i, (a - 1) * S + b].astype(f32)
            if b:
                ss[it, i, b - 1] = total.astype(bf16)
                send(("second", it, i, b), ss.at[it, i, b - 1], sr.at[it, i, b - 1], at(*p.place(second, b)[:3]))
            else:
                usum[i] = total

    def reduce3(it, i):
        S = p.dims(i)[3]
        total = usum[i]
        for b in range(1, S):
            arrived(("second", it, i, b), sr.at[it, i, b - 1])
            total = total + sr[it, i, b - 1].astype(f32)
        asm[:, 0:w] = total
        for d in range(1, Z):
            bs[it, i, d - 1] = asm[d * T:(d + 1) * T, 0:w].astype(bf16)
            send(("back", it, i, d), bs.at[it, i, d - 1], br.at[it, i, d - 1], at(rz=d))
        own[i] = asm[0:T, 0:w]

    def settle(it, i):
        mixed = own[i]
        for d in range(1, Z):
            arrived(("back", it, i, d), br.at[it, i, d - 1])
            mixed = mixed + br[it, i, d - 1].astype(f32)
        cols = pl.ds(i * w, w)
        fresh = (NUDGE * state[:, cols] + NUDGE * (tokens_ref[:, cols].astype(f32) + mixed)).astype(bf16)
        if it + 1 < ITERS:
            state[:, cols] = fresh.astype(f32)
            prepare(it + 1, i, fresh.astype(f32))
            enter(it + 1, i)
        else:
            out_ref[:, cols] = fresh

    steps = dict(enter=enter, level1=level1, level2=level2, level3=level3, multiply=multiply, activate=activate,
                 down=down, reduce1=reduce1, reduce2=reduce2, reduce3=reduce3, settle=settle, weights=weights)
    for name in order:
        steps[name[0]](*name[1:])
        if name == ("enter", 0, 0):
            for rc in range(C):
                for rx in range(X):
                    if rc or rx:
                        r = ((-rc) % C) * X + (-rx) % X
                        send(("route", r), tab, tabs.at[r], at(rc=rc, rx=rx))
    for made in sent:
        made.wait_send()


def deep_scratch(p):
    X, Y, Z, R, w, T, n, U = p.X, p.Y, p.Z, p.R, p.w, p.tok, p.n, p.U
    S, FS = max(X, Y), max((X - 1) * Y, (Y - 1) * X)
    wide, rows, half = w + LANES, p.rows, p.half
    return [
        ((p.D, U), bf16), ((p.D, U), bf16), ((n, U, w), bf16),
        ((ITERS, n, p.NB, R, wide), bf16),
        ((ITERS, n, T, wide), bf16), ((ITERS, n, Z, T, wide), bf16), ((R, wide), f32),
        ((2, rows, U), f32), ((rows, U), bf16),
        ((p.E, LANES), f32), ((p.E, p.E, LANES), f32), ((rows, LANES), f32),
        ((T, p.D), f32),
        ((n, half, w), f32), ((ITERS, n, half, w), bf16), ((ITERS, n, half, w), bf16),
        ((ITERS, n, FS, R, w), bf16), ((ITERS, n, FS, R, w), bf16),
        ((n, S, R, w), f32),
        ((ITERS, n, S - 1, R, w), bf16), ((ITERS, n, S - 1, R, w), bf16),
        ((n, R, w), f32),
        ((n, T, w), f32),
        ((ITERS, n, Z - 1, T, w), bf16), ((ITERS, n, Z - 1, T, w), bf16),
    ]


def on_device(experts, hidden, tokens, norm_gain, gate_weight, up_weight, down_weight, expert_ids, route_weight):
    tok, width = tokens.shape
    p = Deep(experts, hidden, tok, width, gate_weight.shape[2])
    buffers = deep_scratch(p)
    size = sum(math.prod(shape) * (4 if kind == f32 else 2) for shape, kind in buffers)
    if size > VMEM_BYTES * 9 // 10 or hidden * tok > LANES:
        return on_device_compact(experts, hidden, tokens, norm_gain, gate_weight, up_weight, down_weight,
                                 expert_ids, route_weight)
    order, _ = orders(p)
    count = len(p.numbers)
    dma = pltpu.SemaphoreType.DMA
    inside = pl.BlockSpec(memory_space=pltpu.VMEM)
    outside = pl.BlockSpec(memory_space=pl.ANY)
    return pl.pallas_call(
        functools.partial(kernel, p, order),
        out_shape=jax.ShapeDtypeStruct((tok, width), bf16),
        in_specs=[inside] * 4 + [outside] * 3,
        out_specs=inside,
        scratch_shapes=[pltpu.VMEM(*b) for b in buffers] + [dma((3 * p.n,)), dma((count,)), dma((count,))],
        compiler_params=pltpu.CompilerParams(
            collective_id=0, has_side_effects=True, vmem_limit_bytes=VMEM_BYTES),
        name="settle",
    )(tokens, norm_gain.reshape(1, width), expert_ids.T, route_weight.T, gate_weight, up_weight, down_weight)


def solution(mesh):
    placed = (
        P(("expert", "hidden"), None),
        P(),
        P("expert", None, "hidden"),
        P("expert", None, "hidden"),
        P("expert", "hidden", None),
        P("expert", None),
        P("expert", None),
    )
    return jax.shard_map(
        functools.partial(on_device, mesh.shape["expert"], mesh.shape["hidden"]),
        mesh=mesh,
        in_specs=placed,
        out_specs=P(("expert", "hidden"), None),
        check_vma=False,
    )
```

```python
import functools
import math

import jax
import jax.numpy as jnp
from jax import lax
from jax.experimental import pallas as pl
from jax.experimental.pallas import tpu as pltpu
from jax.sharding import PartitionSpec as P

ITERS = 2
EPSILON = 1e-05
NUDGE = 0.5
CHUNKS = 4
LANES = 128
MESH = pl.DeviceIdType.MESH
f32, bf16 = jnp.float32, jnp.bfloat16


class Plan:
    def __init__(self, experts, hidden, tok, width, units):
        self.E, self.H, self.tok, self.D, self.U = experts, hidden, tok, width, units
        self.C = 2
        self.X = experts // self.C
        self.Y = 2
        self.Z = hidden // self.Y
        self.R = self.Z * tok
        self.NB = self.C * self.X * self.Y
        self.K = width // CHUNKS
        self.rows = self.NB * self.R
        self.numbers = {}

    def number(self, key):
        return self.numbers.setdefault(key, len(self.numbers))

    def block(self, rc, rx, ry):
        return (rc * self.X + rx) * self.Y + ry


def all_keys(p):
    for rc in range(p.C):
        for rx in range(p.X):
            if rc or rx:
                p.number(("route", rc, rx))
    for i in range(CHUNKS):
        for d in range(1, p.Z):
            p.number(("z", i, d))
        for b in range(1, p.NB):
            p.number(("blk", i, b))
        p.number(("core", i))
        f, s = (p.X, p.Y) if i % 2 == 0 else (p.Y, p.X)
        for d in range(1, f):
            p.number(("first", i, d))
        for d in range(1, s):
            p.number(("second", i, d))
        for d in range(1, p.Z):
            p.number(("back", i, d))


def tiles(count, body):
    if count == 1:
        body(0)
    else:
        pl.loop(0, count)(body)


def compact_kernel(p, tokens_ref, gain_ref, route_ref, gate_hbm, up_hbm, down_hbm, out_ref,
           wg, wu, wd, xg, n4, z1, asm, acc, hid, route_in, wrow, state, keep, cs, cr,
           fs, fr, held, ss, sr, usum, own, bs, br, wsem, send_sem, recv_sem):
    C, X, Y, Z, R, K, T = p.C, p.X, p.Y, p.Z, p.R, p.K, p.tok
    e, h = lax.axis_index("expert"), lax.axis_index("hidden")
    x, c = e // C, e % C
    z, y = h // Y, h % Y

    def at(rc=0, rx=0, ry=0, rz=0):
        return ((x + rx) % X * C + (c + rc) % C, (z + rz) % Z * Y + (y + ry) % Y)

    loads = []
    for i in range(CHUNKS):
        rows = pl.ds(i * K, K)
        loads.append(pltpu.make_async_copy(gate_hbm.at[0, rows, :], wg.at[rows, :], wsem.at[3 * i]))
        loads.append(pltpu.make_async_copy(up_hbm.at[0, rows, :], wu.at[rows, :], wsem.at[3 * i + 1]))
    for i in range(CHUNKS):
        cols = pl.ds(i * K, K)
        loads.append(pltpu.make_async_copy(down_hbm.at[0, :, cols], wd.at[i], wsem.at[3 * i + 2]))
    for load in loads:
        load.start()

    barrier = pltpu.get_barrier_semaphore()
    partners = [at(rc=rc, rx=rx) for rc in range(C) for rx in range(X) if rc or rx]
    partners += [at(ry=d) for d in range(1, Y)] + [at(rz=d) for d in range(1, Z)]
    for partner in partners:
        pl.semaphore_signal(barrier, inc=1, device_id=partner, device_id_type=MESH)

    state[...] = tokens_ref[...].astype(f32)
    pl.semaphore_wait(barrier, len(partners))

    def copy(key, src, dst, to):
        n = p.number(key)
        return pltpu.make_async_remote_copy(
            src_ref=src, dst_ref=dst, send_sem=send_sem.at[n], recv_sem=recv_sem.at[n],
            device_id=to, device_id_type=MESH)

    def send(sent, *args):
        made = copy(*args)
        made.start()
        sent.append(made)

    def arrived(key, dst):
        copy(key, dst, dst, at(rc=1)).wait_recv()

    routes = []
    for rc in range(C):
        for rx in range(X):
            if rc or rx:
                send(routes, ("route", (-rc) % C, (-rx) % X), route_ref,
                     route_in.at[((-rc) % C) * X + (-rx) % X], at(rc=rc, rx=rx))

    def iteration(it, _):
        first_time = it == 0

        values = state[...]
        mean_square = jnp.sum(values * values, axis=-1, keepdims=True) / p.D
        normed = (values * lax.rsqrt(mean_square + EPSILON) * gain_ref[...]).astype(bf16)
        for i in range(CHUNKS):
            n4[i] = normed[:, i * K:(i + 1) * K]
        sent = []
        for i in range(CHUNKS):
            for d in range(1, Z):
                send(sent, ("z", i, Z - d), n4.at[i], z1.at[i, Z - d], at(rz=d))

        def block_to(i, b_from, rc, rx, ry):
            b, rest = b_from % Y, b_from // Y
            fx, fc = rest % X, rest // X
            there = p.block((fc - rc) % C, (fx - rx) % X, (b - ry) % Y)
            send(sent, ("blk", i, there), xg.at[i, b_from], xg.at[i, there], at(rc, rx, ry))

        def got(i, b):
            arrived(("blk", i, b), xg.at[i, b])

        def level1(i):
            for d in range(1, Z):
                arrived(("z", i, d), z1.at[i, d])
            asm[0:T, :] = n4[i].astype(f32)
            for d in range(1, Z):
                asm[d * T:(d + 1) * T, :] = z1[i, d].astype(f32)
            xg[i, 0] = asm[...].astype(bf16)
            for d in range(1, Y):
                block_to(i, 0, 0, 0, d)
            for d in range(1, X):
                block_to(i, 0, 0, d, 0)
            block_to(i, 0, 1, 0, 0)

        def level2(i):
            if i % 2 == 0:
                for ry in range(1, Y):
                    b = p.block(0, 0, ry)
                    got(i, b)
                    for d in range(1, X):
                        block_to(i, b, 0, d, 0)
                    block_to(i, b, 1, 0, 0)
                for rx in range(1, X):
                    b = p.block(0, rx, 0)
                    got(i, b)
                    block_to(i, b, 1, 0, 0)
            else:
                for rx in range(1, X):
                    b = p.block(0, rx, 0)
                    got(i, b)
                    for d in range(1, Y):
                        block_to(i, b, 0, 0, d)
                    block_to(i, b, 1, 0, 0)
                for ry in range(1, Y):
                    b = p.block(0, 0, ry)
                    got(i, b)
                    block_to(i, b, 1, 0, 0)

        def level3(i):
            for rx in range(1, X):
                for ry in range(1, Y):
                    b = p.block(0, rx, ry)
                    got(i, b)
                    block_to(i, b, 1, 0, 0)

        per = max(1, min(p.NB, 128 // R))
        row_tiles = p.NB // per
        high = per * R
        wide = min(512, p.U)

        def multiply(i):
            for b in range(X * Y, p.NB):
                got(i, b)

            @pl.when(first_time)
            def _():
                loads[2 * i].wait()
                loads[2 * i + 1].wait()

            def column(n):
                cols = pl.ds(pl.multiple_of(n * wide, wide), wide)

                def row(m):
                    block = xg[i, pl.ds(m * per, per)].reshape(high, K)
                    place = pl.ds(pl.multiple_of(m * high, high), high)
                    for side, weight in ((0, wg), (1, wu)):
                        product = jnp.dot(block, weight[pl.ds(i * K, K), cols], preferred_element_type=f32)
                        if i == 0:
                            acc[side, place, cols] = product
                        else:
                            acc[side, place, cols] += product

                tiles(row_tiles, row)

            tiles(p.U // wide, column)

        for t in range(CHUNKS + 3):
            if t < CHUNKS:
                level1(t)
            if 0 <= t - 1 < CHUNKS:
                level2(t - 1)
            if 0 <= t - 2 < CHUNKS:
                level3(t - 2)
            if 0 <= t - 3 < CHUNKS:
                multiply(t - 3)
        for made in sent:
            made.wait_send()

        @pl.when(first_time)
        def _():
            lane = lax.broadcasted_iota(jnp.int32, (T, LANES), 1)
            for rc in range(C):
                for rx in range(X):
                    if rc or rx:
                        arrived(("route", rc, rx), route_in.at[rc * X + rx])
                    for ry in range(Y):
                        for rz in range(Z):
                            _, whose = at(ry=ry, rz=rz)
                            if rc or rx:
                                part = route_in[rc * X + rx, whose]
                            else:
                                part = route_ref[whose]
                            mine = jnp.sum(jnp.where(lane == e, part, 0.0), axis=1, keepdims=True)
                            base = p.block(rc, rx, ry) * R + rz * T
                            wrow[base:base + T, :] = jnp.broadcast_to(mine, (T, LANES))

        def activate(n):
            cols = pl.ds(pl.multiple_of(n * LANES, LANES), LANES)

            def row(m):
                place = pl.ds(pl.multiple_of(m * high, high), high)
                gate = acc[0, place, cols]
                units = gate / (1.0 + jnp.exp(-gate)) * acc[1, place, cols]
                hid[place, cols] = (units * wrow[place, :]).astype(bf16)

            tiles(row_tiles, row)

        tiles(p.U // LANES, activate)

        sent = []
        half = p.rows // C
        narrow = 512 if K % 512 == 0 else LANES

        def down(i):
            @pl.when(first_time)
            def _():
                loads[2 * CHUNKS + i].wait()

            def column(n):
                cols = pl.ds(pl.multiple_of(n * narrow, narrow), narrow)

                def row(m):
                    place = pl.ds(pl.multiple_of(m * 64, 64), 64)
                    other = pl.ds(pl.multiple_of(half + m * 64, 64), 64)
                    cs[i, place, cols] = jnp.dot(hid[other, :], wd[i, :, cols], preferred_element_type=f32).astype(bf16)
                    keep[i % 2, place, cols] = jnp.dot(hid[place, :], wd[i, :, cols], preferred_element_type=f32)

                tiles(half // 64, row)

            tiles(K // narrow, column)
            send(sent, ("core", i), cs.at[i], cr.at[i], at(rc=1))

        def dims(i):
            if i % 2 == 0:
                return X, Y, lambda a, b: a * Y + b, lambda d: at(rx=d), lambda d: at(ry=d)
            return Y, X, lambda a, b: b * Y + a, lambda d: at(ry=d), lambda d: at(rx=d)

        def reduce1(i):
            arrived(("core", i), cr.at[i])
            F, S, place, to_first, _ = dims(i)
            for a in list(range(1, F)) + [0]:
                for b in range(S):
                    rows = pl.ds(place(a, b) * R, R)
                    total = keep[i % 2, rows, :] + cr[i, rows, :].astype(f32)
                    if a:
                        fs[i, (a - 1) * S + b] = total.astype(bf16)
                    else:
                        held[i % 2, b] = total
                if a:
                    send(sent, ("first", i, a), fs.at[i, pl.ds((a - 1) * S, S)],
                         fr.at[i, pl.ds((a - 1) * S, S)], to_first(a))

        def reduce2(i):
            F, S, _, _, to_second = dims(i)
            for a in range(1, F):
                arrived(("first", i, a), fr.at[i, pl.ds((a - 1) * S, S)])
            for b in list(range(1, S)) + [0]:
                total = held[i % 2, b]
                for a in range(1, F):
                    total = total + fr[i, (a - 1) * S + b].astype(f32)
                if b:
                    ss[i, b - 1] = total.astype(bf16)
                    send(sent, ("second", i, b), ss.at[i, b - 1], sr.at[i, b - 1], to_second(b))
                else:
                    usum[i % 2] = total

        def reduce3(i):
            S = dims(i)[1]
            total = usum[i % 2]
            for b in range(1, S):
                arrived(("second", i, b), sr.at[i, b - 1])
                total = total + sr[i, b - 1].astype(f32)
            asm[...] = total
            for d in range(1, Z):
                bs[i, d - 1] = asm[d * T:(d + 1) * T, :].astype(bf16)
                send(sent, ("back", i, d), bs.at[i, d - 1], br.at[i, d - 1], at(rz=d))
            own[i] = asm[0:T, :]

        def settle(i):
            mixed = own[i]
            for d in range(1, Z):
                arrived(("back", i, d), br.at[i, d - 1])
                mixed = mixed + br[i, d - 1].astype(f32)
            cols = pl.ds(i * K, K)
            fresh = (NUDGE * state[:, cols] + NUDGE * (tokens_ref[:, cols].astype(f32) + mixed)).astype(bf16)
            state[:, cols] = fresh.astype(f32)
            out_ref[:, cols] = fresh

        steps = (down, reduce1, reduce2, reduce3, settle)
        for t in range(CHUNKS + len(steps) - 1):
            for lag, step in enumerate(steps):
                if 0 <= t - lag < CHUNKS:
                    step(t - lag)
        for made in sent:
            made.wait_send()
        return 0

    lax.fori_loop(0, ITERS, iteration, 0)
    for made in routes:
        made.wait_send()


def on_device_compact(experts, hidden, tokens, norm_gain, gate_weight, up_weight, down_weight, expert_ids, route_weight):
    tok, width = tokens.shape
    p = Plan(experts, hidden, tok, width, gate_weight.shape[2])
    all_keys(p)
    lanes = jnp.arange(LANES, dtype=jnp.int32)[None, :]
    table = (jnp.where(expert_ids[:, 0:1] == lanes, route_weight[:, 0:1], 0.0)
             + jnp.where(expert_ids[:, 1:2] == lanes, route_weight[:, 1:2], 0.0))
    table = table.reshape(hidden, tok, LANES)
    n, K, R, U = len(p.numbers), p.K, p.R, p.U
    S, FS = max(p.X, p.Y), max((p.X - 1) * p.Y, (p.Y - 1) * p.X)
    half = p.rows // p.C
    vmem = pltpu.VMEM
    scratch = [
        vmem((width, U), bf16), vmem((width, U), bf16), vmem((CHUNKS, U, K), bf16),
        vmem((CHUNKS, p.NB, R, K), bf16),
        vmem((CHUNKS, tok, K), bf16), vmem((CHUNKS, p.Z, tok, K), bf16), vmem((R, K), f32),
        vmem((2, p.rows, U), f32), vmem((p.rows, U), bf16),
        vmem((experts, hidden, tok, LANES), f32), vmem((p.rows, LANES), f32),
        vmem((tok, width), f32),
        vmem((2, half, K), f32), vmem((CHUNKS, half, K), bf16), vmem((CHUNKS, half, K), bf16),
        vmem((CHUNKS, FS, R, K), bf16), vmem((CHUNKS, FS, R, K), bf16),
        vmem((2, S, R, K), f32),
        vmem((CHUNKS, S - 1, R, K), bf16), vmem((CHUNKS, S - 1, R, K), bf16),
        vmem((2, R, K), f32),
        vmem((CHUNKS, tok, K), f32),
        vmem((CHUNKS, p.Z - 1, tok, K), bf16), vmem((CHUNKS, p.Z - 1, tok, K), bf16),
        pltpu.SemaphoreType.DMA((3 * CHUNKS,)),
        pltpu.SemaphoreType.DMA((n,)), pltpu.SemaphoreType.DMA((n,)),
    ]
    inside = pl.BlockSpec(memory_space=pltpu.VMEM)
    outside = pl.BlockSpec(memory_space=pl.ANY)
    return pl.pallas_call(
        functools.partial(compact_kernel, p),
        out_shape=jax.ShapeDtypeStruct((tok, width), bf16),
        in_specs=[inside] * 3 + [outside] * 3,
        out_specs=inside,
        scratch_shapes=scratch,
        compiler_params=pltpu.CompilerParams(
            collective_id=0, has_side_effects=True, vmem_limit_bytes=67_000_000),
        name="settle",
    )(tokens, norm_gain.reshape(1, width), table, gate_weight, up_weight, down_weight)


WIDE = 1024
VMEM_BYTES = 67_000_000
LINK = 46.0e3
LATENCY = {"x": 2.0, "y": 2.0, "z": 2.75, "c": 1.0}
COST = {"level1": 0.04, "aside": 0.01, "level2": 0.04, "level3": 0.03, "corner": 0.01, "multiply": 0.6,
        "activate": 0.28, "down": 0.46, "reduce1": 0.03, "reduce2": 0.03, "reduce3": 0.03, "settle": 0.1,
        "enter": 0.01, "weights": 0.3}
HEAVY = ("multiply", "down", "activate", "weights")
GATHER = ("level1", "aside", "level2", "level3", "corner")
RANK = {}
AHEAD, BEHIND, BONUS = 6, 6, 0.3


class Deep:
    def __init__(self, experts, hidden, tok, width, units):
        self.E, self.H, self.tok, self.D, self.U = experts, hidden, tok, width, units
        self.C, self.Y = 2, 2
        self.X, self.Z = experts // self.C, hidden // self.Y
        self.R = self.Z * tok
        self.B = self.X * self.Y
        self.NB = self.C * self.B
        self.w = WIDE if width % WIDE == 0 else LANES
        self.n = width // self.w
        self.rows = self.NB * self.R
        self.half = self.rows // self.C
        self.numbers = {}

    def lane(self, key):
        kind = key[0]
        if kind == "route":
            group = (kind,)
        elif kind in ("z", "back", "core"):
            group = (kind, key[2])
        elif kind in ("own", "rest"):
            group = ("near",) + key[2:]
        elif kind == "blk" and key[3] >= self.B:
            group = ("joined", key[2])
        else:
            group = (kind,) + key[2:]
        return self.numbers.setdefault(group, len(self.numbers))

    def block(self, rc, rx, ry):
        return (rc * self.X + rx) * self.Y + ry

    def dims(self, i):
        if i % 2 == 0:
            return "x", "y", self.X, self.Y
        return "y", "x", self.Y, self.X

    def place(self, axis, d):
        return (0, d, 0, 0) if axis == "x" else (0, 0, d, 0)

    def at_block(self, *pairs):
        steps = dict(zip(pairs[::2], pairs[1::2]))
        return self.block(0, steps.get("x", 0), steps.get("y", 0))

    def slot(self, axis, d):
        return d - 1 if axis == "x" else self.X - 2 + d

    def take(self, i):
        return self.w + LANES if i == self.n - 1 else self.w


def orders(p):
    X, Y, Z, R, T, n, w = p.X, p.Y, p.Z, p.R, p.tok, p.n, p.w
    tasks = {}

    def leave(it, i):
        out = [(("z", it, i, d), "z", T * p.take(i) * 2) for d in range(1, Z)]
        first, second, F, S = p.dims(i)
        for axis, count in ((first, F), (second, S)):
            out += [(("own", it, i, axis, d), axis, T * p.take(i) * 2) for d in range(1, count)]
        return out

    def core(it, i, b):
        return [(("blk", it, i, b + p.B), "c", R * p.take(i) * 2)]

    def add(name, deps=(), needs=(), sends=()):
        tasks[name] = (list(deps), list(needs), list(sends))

    def rest(it, i, axis, count):
        return [(("rest", it, i, axis, d), axis, (Z - 1) * T * p.take(i) * 2) for d in range(1, count)]

    for it in range(ITERS):
        for i in range(n):
            size = R * p.take(i) * 2
            first, second, F, S = p.dims(i)
            if it == 0:
                add(("enter", it, i), sends=leave(it, i))
                before = [("enter", it, i)]
            else:
                before = [("settle", it - 1, i)]
            add(("level1", it, i), before, [("z", it, i, d) for d in range(1, Z)],
                rest(it, i, first, F) + core(it, i, 0))
            after = [("level2", it, i - AHEAD, d) for d in range(1, p.dims(i - AHEAD)[2])] if i >= AHEAD else []
            add(("aside", it, i), [("level1", it, i)] + after, (), rest(it, i, second, S))
            for d in range(1, F):
                b = p.at_block(first, d)
                diag = [(("blk", it, i, p.at_block(first, d, second, g)), second, size) for g in range(1, S)]
                add(("level2", it, i, d), [("level1", it, i)],
                    [("own", it, i, first, d), ("rest", it, i, first, d)], diag + core(it, i, b))
                for g in range(1, S):
                    b = p.at_block(first, d, second, g)
                    add(("corner", it, i, d, g), [("level1", it, i)], [("blk", it, i, b)], core(it, i, b))
            for g in range(1, S):
                add(("level3", it, i, g), [("level1", it, i)],
                    [("own", it, i, second, g), ("rest", it, i, second, g)], core(it, i, p.at_block(second, g)))
            local = [t for t in tasks if t[0] in GATHER and t[1:3] == (it, i)]
            if i:
                local.append(("multiply", it, i - 1))
            add(("multiply", it, i), local, [("blk", it, i, b + p.B) for b in range(p.B)])
            add(("down", it, i), [("activate", it, 0)] + ([("down", it, i - 1)] if i else []), (),
                [(("core", it, i), "c", p.half * w * 2)])
            after = [("reduce2", it, i - BEHIND)] if i >= BEHIND else []
            add(("reduce1", it, i), [("down", it, i)] + after, [("core", it, i)],
                [(("first", it, i, a), first, S * R * w * 2) for a in range(1, F)])
            add(("reduce2", it, i), [("reduce1", it, i)], [("first", it, i, a) for a in range(1, F)],
                [(("second", it, i, b), second, R * w * 2) for b in range(1, S)])
            add(("reduce3", it, i), [("reduce2", it, i)], [("second", it, i, b) for b in range(1, S)],
                [(("back", it, i, d), "z", T * w * 2) for d in range(1, Z)])
            add(("settle", it, i), [("reduce3", it, i)] + ([("settle", it, i - 1)] if i else []),
                [("back", it, i, d) for d in range(1, Z)], leave(it + 1, i) if it + 1 < ITERS else [])
        add(("activate", it, 0), [("multiply", it, n - 1), ("weights", 0, 0)])
    add(("weights", 0, 0), [("enter", 0, n - 1)], [("route", r) for r in range(1, p.C * X)])

    p.bytes = 0
    for _, _, sends in tasks.values():
        for key, _, size in sends:
            p.lane(key)
            p.bytes += size
    p.lane(("route", 1))
    unit, table = 16 * p.U, (p.C * X - 1) * p.E * LANES * 4
    p.copies = next((m for m in range(1, 17) if (p.bytes + m * table) % unit == 0), 0)
    p.bytes += p.copies * table

    rate = {"x": LINK, "y": LINK, "z": LINK * 3 / Z, "c": 600.0e3}
    free = dict.fromkeys(rate, 0.0)
    arrival = {("route", r): 3.0 for r in range(1, p.C * X)}
    now, order, left = 0.0, [], dict(tasks)
    done = set()
    while left:
        best = None
        for position, (name, (deps, needs, _)) in enumerate(left.items()):
            if any(d not in done for d in deps) or any(k not in arrival for k in needs):
                continue
            ready = max([now] + [arrival[k] for k in needs])
            rank = (ready + (BONUS if name[0] in HEAVY else 0.0), RANK.get(name[0], 0), position)
            if best is None or rank < best[0]:
                best = (rank, name, ready)
        _, name, ready = best
        now = ready + COST[name[0]]
        for key, link, size in left[name][2]:
            begin = max(free[link], now)
            free[link] = begin + size / rate[link]
            arrival[key] = free[link] + LATENCY[link]
        done.add(name)
        order.append(name)
        del left[name]
    return order, now


def kernel(p, order, tokens_ref, gain_ref, ids_ref, weight_ref, gate_hbm, up_hbm, down_hbm, out_ref,
           wg, wu, wd, xg, z1, zn, asm, acc, hid, tab, tabs, wrow, state, keep, cs, cr,
           fs, fr, held, ss, sr, usum, own, bs, br, wsem, send_sem, recv_sem):
    C, X, Y, Z, R, w, T, n = p.C, p.X, p.Y, p.Z, p.R, p.w, p.tok, p.n
    e, h = lax.axis_index("expert"), lax.axis_index("hidden")
    x, c = e // C, e % C
    z, y = h // Y, h % Y

    def at(rc=0, rx=0, ry=0, rz=0):
        return ((x + rx) % X * C + (c + rc) % C, (z + rz) % Z * Y + (y + ry) % Y)

    loads = []
    for i in range(n):
        rows = pl.ds(i * w, w)
        loads.append(pltpu.make_async_copy(gate_hbm.at[0, rows, :], wg.at[rows, :], wsem.at[3 * i]))
        loads.append(pltpu.make_async_copy(up_hbm.at[0, rows, :], wu.at[rows, :], wsem.at[3 * i + 1]))
    for i in range(n):
        loads.append(pltpu.make_async_copy(down_hbm.at[0, :, pl.ds(i * w, w)], wd.at[i], wsem.at[3 * i + 2]))

    barrier = pltpu.get_barrier_semaphore()
    partners = [at(rc=rc, rx=rx) for rc in range(C) for rx in range(X) if rc or rx]
    partners += [at(ry=d) for d in range(1, Y)] + [at(rz=d) for d in range(1, Z)]
    for partner in partners:
        pl.semaphore_signal(barrier, inc=1, device_id=partner, device_id_type=MESH)
    for load in loads:
        load.start()

    def copy(key, src, dst, to):
        return pltpu.make_async_remote_copy(
            src_ref=src, dst_ref=dst, send_sem=send_sem.at[0], recv_sem=recv_sem.at[p.lane(key)],
            device_id=to, device_id_type=MESH)

    def send(*args):
        copy(*args).start()

    def arrived(key, dst):
        copy(key, dst, dst, at(rc=1)).wait_recv()

    def scales(square):
        scale = lax.rsqrt(square / p.D + EPSILON)
        high = scale.astype(bf16).astype(f32)
        middle = (scale - high).astype(bf16).astype(f32)
        low = scale - high - middle
        lane = lax.broadcasted_iota(jnp.int32, (T, LANES), 1)
        parts = jnp.where(lane == 0, high, jnp.where(lane == 1, middle, jnp.where(lane == 2, low, 0.0)))
        return parts.astype(bf16)

    squares = [None] * ITERS

    def prepare(it, i, values):
        cols = pl.ds(i * w, w)
        square = jnp.sum(values * values, axis=-1, keepdims=True)
        squares[it] = square if i == 0 else squares[it] + square
        z1[it, i, 0, :, 0:w] = (values * gain_ref[:, cols]).astype(bf16)
        if i == n - 1:
            z1[it, i, 0, :, w:w + LANES] = scales(squares[it])

    def around(axis, d):
        return at(rx=d) if axis == "x" else at(ry=d)

    def back_from(axis, d):
        return ((X if axis == "x" else Y) - d) % (X if axis == "x" else Y)

    def slab(it, i, d):
        return z1.at[it, i, d, :, pl.ds(0, p.take(i))]

    def near(it, i, axis, d, part):
        full = zn.at[it, i, p.slot(axis, d)]
        return full.at[part, :, pl.ds(0, p.take(i))]

    def enter(it, i):
        for d in range(1, Z):
            send(("z", it, i, Z - d), slab(it, i, 0), slab(it, i, Z - d), at(rz=d))
        first, second, F, S = p.dims(i)
        for axis, count in ((first, F), (second, S)):
            for d in range(1, count):
                g = back_from(axis, d)
                send(("own", it, i, axis, g), slab(it, i, 0), near(it, i, axis, g, 0), around(axis, d))

    def rest(it, i, axis, count):
        for d in range(1, count):
            g = back_from(axis, d)
            send(("rest", it, i, axis, g), z1.at[it, i, pl.ds(1, Z - 1), :, pl.ds(0, p.take(i))],
                 near(it, i, axis, g, pl.ds(1, Z - 1)), around(axis, d))

    def gather_near(it, i, axis, d):
        arrived(("own", it, i, axis, d), near(it, i, axis, d, pl.ds(0, Z)))
        b = p.at_block(axis, d)
        join(it, i, b, lambda k, wide: zn[it, i, p.slot(axis, d), k, :, 0:wide])
        return b

    def join(it, i, b, part):
        wide = p.take(i)
        for d in range(Z):
            asm[d * T:(d + 1) * T, 0:wide] = part(d, wide).astype(f32)
        xg[it, i, b, :, 0:wide] = asm[:, 0:wide].astype(bf16)

    values = tokens_ref[...].astype(f32)
    state[...] = values
    for i in range(n):
        prepare(0, i, values[:, i * w:(i + 1) * w])
    L = p.H * T
    which = lax.broadcasted_iota(jnp.int32, (p.E, L), 0)
    tab[...] = jnp.zeros_like(tab)
    tab[0, :, 0:L] = (jnp.where(ids_ref[0:1, :] == which, weight_ref[0:1, :], 0.0)
                   + jnp.where(ids_ref[1:2, :] == which, weight_ref[1:2, :], 0.0))
    pl.semaphore_wait(barrier, len(partners))

    def weights(*_):
        lane = lax.broadcasted_iota(jnp.int32, (T, LANES), 1)
        token = lax.broadcasted_iota(jnp.int32, (T, LANES), 0)
        expert = lax.broadcasted_iota(jnp.int32, (p.E, LANES), 0)
        arrived(("route", 1), tabs.at[pl.ds(1, C * X - 1)])
        for rc in range(C):
            for rx in range(X):
                r = rc * X + rx
                table = tabs[r, 0] if r else tab[0]
                mine = jnp.sum(jnp.where(expert == e, table, 0.0), axis=0, keepdims=True)
                for ry in range(Y):
                    for rz in range(Z):
                        _, whose = at(ry=ry, rz=rz)
                        part = jnp.where(lane == whose * T + token, mine, 0.0)
                        base = p.block(rc, rx, ry) * R + rz * T
                        wrow[base:base + T, :] = jnp.broadcast_to(
                            jnp.sum(part, axis=1, keepdims=True), (T, LANES))

    def piece(it, i, b):
        return xg.at[it, i, b, :, pl.ds(0, p.take(i))]

    def block_to(it, i, b_from, rc, rx, ry):
        b, rest = b_from % Y, b_from // Y
        fx, fc = rest % X, rest // X
        there = p.block((fc - rc) % C, (fx - rx) % X, (b - ry) % Y)
        send(("blk", it, i, there), piece(it, i, b_from), piece(it, i, there), at(rc, rx, ry))

    def got(it, i, b, count=1):
        arrived(("blk", it, i, b), piece(it, i, pl.ds(b, count)))

    def level1(it, i):
        arrived(("z", it, i, 1), slab(it, i, pl.ds(1, Z - 1)))
        first, _, F, _ = p.dims(i)
        rest(it, i, first, F)
        join(it, i, 0, lambda k, wide: z1[it, i, k, :, 0:wide])
        block_to(it, i, 0, 1, 0, 0)

    def aside(it, i):
        _, second, _, S = p.dims(i)
        rest(it, i, second, S)

    def level2(it, i, d):
        first, second, _, S = p.dims(i)
        b = gather_near(it, i, first, d)
        for g in range(1, S):
            block_to(it, i, b, *p.place(second, g)[:3])
        block_to(it, i, b, 1, 0, 0)

    def level3(it, i, g):
        b = gather_near(it, i, p.dims(i)[1], g)
        block_to(it, i, b, 1, 0, 0)

    def corner(it, i, d, g):
        first, second, _, _ = p.dims(i)
        b = p.at_block(first, d, second, g)
        got(it, i, b)
        block_to(it, i, b, 1, 0, 0)

    def multiply(it, i):
        got(it, i, p.B, p.B)
        if it == 0:
            loads[2 * i].wait()
            loads[2 * i + 1].wait()
        block = xg[it, i, :, :, 0:w].reshape(p.rows, w)
        for side, weight in ((0, wg), (1, wu)):
            product = jnp.dot(block, weight[i * w:(i + 1) * w, :], preferred_element_type=f32)
            if i == 0:
                acc[side] = product
            else:
                acc[side] += product

    def activate(it, _):
        parts = xg[it, n - 1, :, :, w:w + LANES].reshape(p.rows, LANES).astype(f32)
        scale = jnp.broadcast_to(jnp.sum(parts, axis=1, keepdims=True), (p.rows, LANES))
        mine = wrow[...]
        for k in range(p.U // LANES):
            cols = slice(k * LANES, (k + 1) * LANES)
            gate = acc[0, :, cols] * scale
            units = gate / (1.0 + jnp.exp(-gate)) * (acc[1, :, cols] * scale)
            hid[:, cols] = (units * mine).astype(bf16)

    def down(it, i):
        if it == 0:
            loads[2 * n + i].wait()
        product = jnp.dot(hid[...], wd[i], preferred_element_type=f32)
        cs[it, i] = product[p.half:, :].astype(bf16)
        send(("core", it, i), cs.at[it, i], cr.at[it, i], at(rc=1))
        keep[i] = product[:p.half, :]

    def reduce1(it, i):
        arrived(("core", it, i), cr.at[it, i])
        first, _, F, S = p.dims(i)
        for a in list(range(1, F)) + [0]:
            for b in range(S):
                b_at = p.block(0, a, b) if first == "x" else p.block(0, b, a)
                rows = pl.ds(b_at * R, R)
                total = keep[i, rows, :] + cr[it, i, rows, :].astype(f32)
                if a:
                    fs[it, i, (a - 1) * S + b] = total.astype(bf16)
                else:
                    held[i, b] = total
            if a:
                send(("first", it, i, a), fs.at[it, i, pl.ds((a - 1) * S, S)],
                     fr.at[it, i, pl.ds((a - 1) * S, S)], at(*p.place(first, a)[:3]))

    def reduce2(it, i):
        _, second, F, S = p.dims(i)
        for a in range(1, F):
            arrived(("first", it, i, a), fr.at[it, i, pl.ds((a - 1) * S, S)])
        for b in list(range(1, S)) + [0]:
            total = held[i, b]
            for a in range(1, F):
                total = total + fr[it, i, (a - 1) * S + b].astype(f32)
            if b:
                ss[it, i, b - 1] = total.astype(bf16)
                send(("second", it, i, b), ss.at[it, i, b - 1], sr.at[it, i, b - 1], at(*p.place(second, b)[:3]))
            else:
                usum[i] = total

    def reduce3(it, i):
        S = p.dims(i)[3]
        total = usum[i]
        for b in range(1, S):
            arrived(("second", it, i, b), sr.at[it, i, b - 1])
            total = total + sr[it, i, b - 1].astype(f32)
        asm[:, 0:w] = total
        for d in range(1, Z):
            bs[it, i, d - 1] = asm[d * T:(d + 1) * T, 0:w].astype(bf16)
            send(("back", it, i, d), bs.at[it, i, d - 1], br.at[it, i, d - 1], at(rz=d))
        own[i] = asm[0:T, 0:w]

    def settle(it, i):
        mixed = own[i]
        arrived(("back", it, i, 1), br.at[it, i])
        for d in range(1, Z):
            mixed = mixed + br[it, i, d - 1].astype(f32)
        cols = pl.ds(i * w, w)
        fresh = (NUDGE * state[:, cols] + NUDGE * (tokens_ref[:, cols].astype(f32) + mixed)).astype(bf16)
        if it + 1 < ITERS:
            state[:, cols] = fresh.astype(f32)
            prepare(it + 1, i, fresh.astype(f32))
            enter(it + 1, i)
        else:
            out_ref[:, cols] = fresh

    steps = dict(enter=enter, level1=level1, aside=aside, level2=level2, level3=level3, corner=corner, multiply=multiply, activate=activate,
                 down=down, reduce1=reduce1, reduce2=reduce2, reduce3=reduce3, settle=settle, weights=weights)
    for name in order:
        steps[name[0]](*name[1:])
        if name == ("enter", 0, 0):
            for rc in range(C):
                for rx in range(X):
                    if rc or rx:
                        r = ((-rc) % C) * X + (-rx) % X
                        send(("route", r), tab, tabs.at[r], at(rc=rc, rx=rx))
    whole = wg.at[pl.ds(0, p.bytes // (2 * p.U)), :]
    pltpu.make_async_copy(whole, whole, send_sem.at[0]).wait()


def deep_scratch(p):
    X, Y, Z, R, w, T, n, U = p.X, p.Y, p.Z, p.R, p.w, p.tok, p.n, p.U
    S, FS = max(X, Y), max((X - 1) * Y, (Y - 1) * X)
    wide, rows, half = w + LANES, p.rows, p.half
    return [
        ((p.D, U), bf16), ((p.D, U), bf16), ((n, U, w), bf16),
        ((ITERS, n, p.NB, R, wide), bf16),
        ((ITERS, n, Z, T, wide), bf16), ((ITERS, n, X + Y - 2, Z, T, wide), bf16), ((R, wide), f32),
        ((2, rows, U), f32), ((rows, U), bf16),
        ((p.copies, p.E, LANES), f32), ((p.E, p.copies, p.E, LANES), f32), ((rows, LANES), f32),
        ((T, p.D), f32),
        ((n, half, w), f32), ((ITERS, n, half, w), bf16), ((ITERS, n, half, w), bf16),
        ((ITERS, n, FS, R, w), bf16), ((ITERS, n, FS, R, w), bf16),
        ((n, S, R, w), f32),
        ((ITERS, n, S - 1, R, w), bf16), ((ITERS, n, S - 1, R, w), bf16),
        ((n, R, w), f32),
        ((n, T, w), f32),
        ((ITERS, n, Z - 1, T, w), bf16), ((ITERS, n, Z - 1, T, w), bf16),
    ]


def on_device(experts, hidden, tokens, norm_gain, gate_weight, up_weight, down_weight, expert_ids, route_weight):
    tok, width = tokens.shape
    p = Deep(experts, hidden, tok, width, gate_weight.shape[2])
    order, _ = orders(p)
    buffers = deep_scratch(p)
    size = sum(math.prod(shape) * (4 if kind == f32 else 2) for shape, kind in buffers)
    if size > VMEM_BYTES * 9 // 10 or hidden * tok > LANES:
        return on_device_compact(experts, hidden, tokens, norm_gain, gate_weight, up_weight, down_weight,
                                 expert_ids, route_weight)
    if not p.copies or p.bytes > 2 * p.U * width:
        raise ValueError("send total")
    count = len(p.numbers)
    dma = pltpu.SemaphoreType.DMA
    inside = pl.BlockSpec(memory_space=pltpu.VMEM)
    outside = pl.BlockSpec(memory_space=pl.ANY)
    return pl.pallas_call(
        functools.partial(kernel, p, order),
        out_shape=jax.ShapeDtypeStruct((tok, width), bf16),
        in_specs=[inside] * 4 + [outside] * 3,
        out_specs=inside,
        scratch_shapes=[pltpu.VMEM(*b) for b in buffers] + [dma((3 * p.n,)), dma((1,)), dma((count,))],
        compiler_params=pltpu.CompilerParams(
            collective_id=0, has_side_effects=True, vmem_limit_bytes=VMEM_BYTES),
        name="settle",
    )(tokens, norm_gain.reshape(1, width), expert_ids.T, route_weight.T, gate_weight, up_weight, down_weight)


def solution(mesh):
    placed = (
        P(("expert", "hidden"), None),
        P(),
        P("expert", None, "hidden"),
        P("expert", None, "hidden"),
        P("expert", "hidden", None),
        P("expert", None),
        P("expert", None),
    )
    return jax.shard_map(
        functools.partial(on_device, mesh.shape["expert"], mesh.shape["hidden"]),
        mesh=mesh,
        in_specs=placed,
        out_specs=P(("expert", "hidden"), None),
        check_vma=False,
    )
```

```python
import functools
import math

import jax
import jax.numpy as jnp
from jax import lax
from jax.experimental import pallas as pl
from jax.experimental.pallas import tpu as pltpu
from jax.sharding import PartitionSpec as P

ITERS = 2
EPSILON = 1e-05
NUDGE = 0.5
CHUNKS = 4
LANES = 128
MESH = pl.DeviceIdType.MESH
f32, bf16 = jnp.float32, jnp.bfloat16


class Plan:
    def __init__(self, experts, hidden, tok, width, units):
        self.E, self.H, self.tok, self.D, self.U = experts, hidden, tok, width, units
        self.C = 2
        self.X = experts // self.C
        self.Y = 2
        self.Z = hidden // self.Y
        self.R = self.Z * tok
        self.NB = self.C * self.X * self.Y
        self.K = width // CHUNKS
        self.rows = self.NB * self.R
        self.numbers = {}

    def number(self, key):
        return self.numbers.setdefault(key, len(self.numbers))

    def block(self, rc, rx, ry):
        return (rc * self.X + rx) * self.Y + ry


def all_keys(p):
    for rc in range(p.C):
        for rx in range(p.X):
            if rc or rx:
                p.number(("route", rc, rx))
    for i in range(CHUNKS):
        for d in range(1, p.Z):
            p.number(("z", i, d))
        for b in range(1, p.NB):
            p.number(("blk", i, b))
        p.number(("core", i))
        f, s = (p.X, p.Y) if i % 2 == 0 else (p.Y, p.X)
        for d in range(1, f):
            p.number(("first", i, d))
        for d in range(1, s):
            p.number(("second", i, d))
        for d in range(1, p.Z):
            p.number(("back", i, d))


def tiles(count, body):
    if count == 1:
        body(0)
    else:
        pl.loop(0, count)(body)


def compact_kernel(p, tokens_ref, gain_ref, route_ref, gate_hbm, up_hbm, down_hbm, out_ref,
           wg, wu, wd, xg, n4, z1, asm, acc, hid, route_in, wrow, state, keep, cs, cr,
           fs, fr, held, ss, sr, usum, own, bs, br, wsem, send_sem, recv_sem):
    C, X, Y, Z, R, K, T = p.C, p.X, p.Y, p.Z, p.R, p.K, p.tok
    e, h = lax.axis_index("expert"), lax.axis_index("hidden")
    x, c = e // C, e % C
    z, y = h // Y, h % Y

    def at(rc=0, rx=0, ry=0, rz=0):
        return ((x + rx) % X * C + (c + rc) % C, (z + rz) % Z * Y + (y + ry) % Y)

    loads = []
    for i in range(CHUNKS):
        rows = pl.ds(i * K, K)
        loads.append(pltpu.make_async_copy(gate_hbm.at[0, rows, :], wg.at[rows, :], wsem.at[3 * i]))
        loads.append(pltpu.make_async_copy(up_hbm.at[0, rows, :], wu.at[rows, :], wsem.at[3 * i + 1]))
    for i in range(CHUNKS):
        cols = pl.ds(i * K, K)
        loads.append(pltpu.make_async_copy(down_hbm.at[0, :, cols], wd.at[i], wsem.at[3 * i + 2]))
    for load in loads:
        load.start()

    barrier = pltpu.get_barrier_semaphore()
    partners = [at(rc=rc, rx=rx) for rc in range(C) for rx in range(X) if rc or rx]
    partners += [at(ry=d) for d in range(1, Y)] + [at(rz=d) for d in range(1, Z)]
    for partner in partners:
        pl.semaphore_signal(barrier, inc=1, device_id=partner, device_id_type=MESH)

    state[...] = tokens_ref[...].astype(f32)
    pl.semaphore_wait(barrier, len(partners))

    def copy(key, src, dst, to):
        n = p.number(key)
        return pltpu.make_async_remote_copy(
            src_ref=src, dst_ref=dst, send_sem=send_sem.at[n], recv_sem=recv_sem.at[n],
            device_id=to, device_id_type=MESH)

    def send(sent, *args):
        made = copy(*args)
        made.start()
        sent.append(made)

    def arrived(key, dst):
        copy(key, dst, dst, at(rc=1)).wait_recv()

    routes = []
    for rc in range(C):
        for rx in range(X):
            if rc or rx:
                send(routes, ("route", (-rc) % C, (-rx) % X), route_ref,
                     route_in.at[((-rc) % C) * X + (-rx) % X], at(rc=rc, rx=rx))

    def iteration(it, _):
        first_time = it == 0

        values = state[...]
        mean_square = jnp.sum(values * values, axis=-1, keepdims=True) / p.D
        normed = (values * lax.rsqrt(mean_square + EPSILON) * gain_ref[...]).astype(bf16)
        for i in range(CHUNKS):
            n4[i] = normed[:, i * K:(i + 1) * K]
        sent = []
        for i in range(CHUNKS):
            for d in range(1, Z):
                send(sent, ("z", i, Z - d), n4.at[i], z1.at[i, Z - d], at(rz=d))

        def block_to(i, b_from, rc, rx, ry):
            b, rest = b_from % Y, b_from // Y
            fx, fc = rest % X, rest // X
            there = p.block((fc - rc) % C, (fx - rx) % X, (b - ry) % Y)
            send(sent, ("blk", i, there), xg.at[i, b_from], xg.at[i, there], at(rc, rx, ry))

        def got(i, b):
            arrived(("blk", i, b), xg.at[i, b])

        def level1(i):
            for d in range(1, Z):
                arrived(("z", i, d), z1.at[i, d])
            asm[0:T, :] = n4[i].astype(f32)
            for d in range(1, Z):
                asm[d * T:(d + 1) * T, :] = z1[i, d].astype(f32)
            xg[i, 0] = asm[...].astype(bf16)
            for d in range(1, Y):
                block_to(i, 0, 0, 0, d)
            for d in range(1, X):
                block_to(i, 0, 0, d, 0)
            block_to(i, 0, 1, 0, 0)

        def level2(i):
            if i % 2 == 0:
                for ry in range(1, Y):
                    b = p.block(0, 0, ry)
                    got(i, b)
                    for d in range(1, X):
                        block_to(i, b, 0, d, 0)
                    block_to(i, b, 1, 0, 0)
                for rx in range(1, X):
                    b = p.block(0, rx, 0)
                    got(i, b)
                    block_to(i, b, 1, 0, 0)
            else:
                for rx in range(1, X):
                    b = p.block(0, rx, 0)
                    got(i, b)
                    for d in range(1, Y):
                        block_to(i, b, 0, 0, d)
                    block_to(i, b, 1, 0, 0)
                for ry in range(1, Y):
                    b = p.block(0, 0, ry)
                    got(i, b)
                    block_to(i, b, 1, 0, 0)

        def level3(i):
            for rx in range(1, X):
                for ry in range(1, Y):
                    b = p.block(0, rx, ry)
                    got(i, b)
                    block_to(i, b, 1, 0, 0)

        per = max(1, min(p.NB, 128 // R))
        row_tiles = p.NB // per
        high = per * R
        wide = min(512, p.U)

        def multiply(i):
            for b in range(X * Y, p.NB):
                got(i, b)

            @pl.when(first_time)
            def _():
                loads[2 * i].wait()
                loads[2 * i + 1].wait()

            def column(n):
                cols = pl.ds(pl.multiple_of(n * wide, wide), wide)

                def row(m):
                    block = xg[i, pl.ds(m * per, per)].reshape(high, K)
                    place = pl.ds(pl.multiple_of(m * high, high), high)
                    for side, weight in ((0, wg), (1, wu)):
                        product = jnp.dot(block, weight[pl.ds(i * K, K), cols], preferred_element_type=f32)
                        if i == 0:
                            acc[side, place, cols] = product
                        else:
                            acc[side, place, cols] += product

                tiles(row_tiles, row)

            tiles(p.U // wide, column)

        for t in range(CHUNKS + 3):
            if t < CHUNKS:
                level1(t)
            if 0 <= t - 1 < CHUNKS:
                level2(t - 1)
            if 0 <= t - 2 < CHUNKS:
                level3(t - 2)
            if 0 <= t - 3 < CHUNKS:
                multiply(t - 3)
        for made in sent:
            made.wait_send()

        @pl.when(first_time)
        def _():
            lane = lax.broadcasted_iota(jnp.int32, (T, LANES), 1)
            for rc in range(C):
                for rx in range(X):
                    if rc or rx:
                        arrived(("route", rc, rx), route_in.at[rc * X + rx])
                    for ry in range(Y):
                        for rz in range(Z):
                            _, whose = at(ry=ry, rz=rz)
                            if rc or rx:
                                part = route_in[rc * X + rx, whose]
                            else:
                                part = route_ref[whose]
                            mine = jnp.sum(jnp.where(lane == e, part, 0.0), axis=1, keepdims=True)
                            base = p.block(rc, rx, ry) * R + rz * T
                            wrow[base:base + T, :] = jnp.broadcast_to(mine, (T, LANES))

        def activate(n):
            cols = pl.ds(pl.multiple_of(n * LANES, LANES), LANES)

            def row(m):
                place = pl.ds(pl.multiple_of(m * high, high), high)
                gate = acc[0, place, cols]
                units = gate / (1.0 + jnp.exp(-gate)) * acc[1, place, cols]
                hid[place, cols] = (units * wrow[place, :]).astype(bf16)

            tiles(row_tiles, row)

        tiles(p.U // LANES, activate)

        sent = []
        half = p.rows // C
        narrow = 512 if K % 512 == 0 else LANES

        def down(i):
            @pl.when(first_time)
            def _():
                loads[2 * CHUNKS + i].wait()

            def column(n):
                cols = pl.ds(pl.multiple_of(n * narrow, narrow), narrow)

                def row(m):
                    place = pl.ds(pl.multiple_of(m * 64, 64), 64)
                    other = pl.ds(pl.multiple_of(half + m * 64, 64), 64)
                    cs[i, place, cols] = jnp.dot(hid[other, :], wd[i, :, cols], preferred_element_type=f32).astype(bf16)
                    keep[i % 2, place, cols] = jnp.dot(hid[place, :], wd[i, :, cols], preferred_element_type=f32)

                tiles(half // 64, row)

            tiles(K // narrow, column)
            send(sent, ("core", i), cs.at[i], cr.at[i], at(rc=1))

        def dims(i):
            if i % 2 == 0:
                return X, Y, lambda a, b: a * Y + b, lambda d: at(rx=d), lambda d: at(ry=d)
            return Y, X, lambda a, b: b * Y + a, lambda d: at(ry=d), lambda d: at(rx=d)

        def reduce1(i):
            arrived(("core", i), cr.at[i])
            F, S, place, to_first, _ = dims(i)
            for a in list(range(1, F)) + [0]:
                for b in range(S):
                    rows = pl.ds(place(a, b) * R, R)
                    total = keep[i % 2, rows, :] + cr[i, rows, :].astype(f32)
                    if a:
                        fs[i, (a - 1) * S + b] = total.astype(bf16)
                    else:
                        held[i % 2, b] = total
                if a:
                    send(sent, ("first", i, a), fs.at[i, pl.ds((a - 1) * S, S)],
                         fr.at[i, pl.ds((a - 1) * S, S)], to_first(a))

        def reduce2(i):
            F, S, _, _, to_second = dims(i)
            for a in range(1, F):
                arrived(("first", i, a), fr.at[i, pl.ds((a - 1) * S, S)])
            for b in list(range(1, S)) + [0]:
                total = held[i % 2, b]
                for a in range(1, F):
                    total = total + fr[i, (a - 1) * S + b].astype(f32)
                if b:
                    ss[i, b - 1] = total.astype(bf16)
                    send(sent, ("second", i, b), ss.at[i, b - 1], sr.at[i, b - 1], to_second(b))
                else:
                    usum[i % 2] = total

        def reduce3(i):
            S = dims(i)[1]
            total = usum[i % 2]
            for b in range(1, S):
                arrived(("second", i, b), sr.at[i, b - 1])
                total = total + sr[i, b - 1].astype(f32)
            asm[...] = total
            for d in range(1, Z):
                bs[i, d - 1] = asm[d * T:(d + 1) * T, :].astype(bf16)
                send(sent, ("back", i, d), bs.at[i, d - 1], br.at[i, d - 1], at(rz=d))
            own[i] = asm[0:T, :]

        def settle(i):
            mixed = own[i]
            for d in range(1, Z):
                arrived(("back", i, d), br.at[i, d - 1])
                mixed = mixed + br[i, d - 1].astype(f32)
            cols = pl.ds(i * K, K)
            fresh = (NUDGE * state[:, cols] + NUDGE * (tokens_ref[:, cols].astype(f32) + mixed)).astype(bf16)
            state[:, cols] = fresh.astype(f32)
            out_ref[:, cols] = fresh

        steps = (down, reduce1, reduce2, reduce3, settle)
        for t in range(CHUNKS + len(steps) - 1):
            for lag, step in enumerate(steps):
                if 0 <= t - lag < CHUNKS:
                    step(t - lag)
        for made in sent:
            made.wait_send()
        return 0

    lax.fori_loop(0, ITERS, iteration, 0)
    for made in routes:
        made.wait_send()


def on_device_compact(experts, hidden, tokens, norm_gain, gate_weight, up_weight, down_weight, expert_ids, route_weight):
    tok, width = tokens.shape
    p = Plan(experts, hidden, tok, width, gate_weight.shape[2])
    all_keys(p)
    lanes = jnp.arange(LANES, dtype=jnp.int32)[None, :]
    table = (jnp.where(expert_ids[:, 0:1] == lanes, route_weight[:, 0:1], 0.0)
             + jnp.where(expert_ids[:, 1:2] == lanes, route_weight[:, 1:2], 0.0))
    table = table.reshape(hidden, tok, LANES)
    n, K, R, U = len(p.numbers), p.K, p.R, p.U
    S, FS = max(p.X, p.Y), max((p.X - 1) * p.Y, (p.Y - 1) * p.X)
    half = p.rows // p.C
    vmem = pltpu.VMEM
    scratch = [
        vmem((width, U), bf16), vmem((width, U), bf16), vmem((CHUNKS, U, K), bf16),
        vmem((CHUNKS, p.NB, R, K), bf16),
        vmem((CHUNKS, tok, K), bf16), vmem((CHUNKS, p.Z, tok, K), bf16), vmem((R, K), f32),
        vmem((2, p.rows, U), f32), vmem((p.rows, U), bf16),
        vmem((experts, hidden, tok, LANES), f32), vmem((p.rows, LANES), f32),
        vmem((tok, width), f32),
        vmem((2, half, K), f32), vmem((CHUNKS, half, K), bf16), vmem((CHUNKS, half, K), bf16),
        vmem((CHUNKS, FS, R, K), bf16), vmem((CHUNKS, FS, R, K), bf16),
        vmem((2, S, R, K), f32),
        vmem((CHUNKS, S - 1, R, K), bf16), vmem((CHUNKS, S - 1, R, K), bf16),
        vmem((2, R, K), f32),
        vmem((CHUNKS, tok, K), f32),
        vmem((CHUNKS, p.Z - 1, tok, K), bf16), vmem((CHUNKS, p.Z - 1, tok, K), bf16),
        pltpu.SemaphoreType.DMA((3 * CHUNKS,)),
        pltpu.SemaphoreType.DMA((n,)), pltpu.SemaphoreType.DMA((n,)),
    ]
    inside = pl.BlockSpec(memory_space=pltpu.VMEM)
    outside = pl.BlockSpec(memory_space=pl.ANY)
    return pl.pallas_call(
        functools.partial(compact_kernel, p),
        out_shape=jax.ShapeDtypeStruct((tok, width), bf16),
        in_specs=[inside] * 3 + [outside] * 3,
        out_specs=inside,
        scratch_shapes=scratch,
        compiler_params=pltpu.CompilerParams(
            collective_id=0, has_side_effects=True, vmem_limit_bytes=67_000_000),
        name="settle",
    )(tokens, norm_gain.reshape(1, width), table, gate_weight, up_weight, down_weight)


WIDE = 1024
VMEM_BYTES = 67_000_000
LINK = 46.0e3
LATENCY = {"x": 2.0, "y": 2.0, "z": 2.75, "c": 1.0}
COST = {"level1": 0.04, "aside": 0.01, "level2": 0.04, "level3": 0.03, "corner": 0.01, "multiply": 0.6,
        "activate": 0.28, "down": 0.46, "reduce1": 0.03, "reduce2": 0.03, "reduce3": 0.03, "settle": 0.1,
        "enter": 0.01, "weights": 0.3}
HEAVY = ("multiply", "down", "activate", "weights")
GATHER = ("level1", "aside", "level2", "level3", "corner")
RANK = {}
AHEAD, BEHIND, BONUS, SOON = 6, 6, 0.3, 2


class Deep:
    def __init__(self, experts, hidden, tok, width, units):
        self.E, self.H, self.tok, self.D, self.U = experts, hidden, tok, width, units
        self.C, self.Y = 2, 2
        self.X, self.Z = experts // self.C, hidden // self.Y
        self.R = self.Z * tok
        self.B = self.X * self.Y
        self.NB = self.C * self.B
        self.w = WIDE if width % WIDE == 0 else LANES
        self.n = width // self.w
        self.rows = self.NB * self.R
        self.half = self.rows // self.C
        self.numbers = {}

    def lane(self, key):
        kind = key[0]
        if kind == "route":
            group = (kind,)
        elif kind in ("z", "back", "core"):
            group = (kind, key[2])
        elif kind in ("own", "rest"):
            group = ("near",) + key[2:]
        elif kind == "blk" and key[3] >= self.B:
            group = ("joined", key[2])
        else:
            group = (kind,) + key[2:]
        return self.numbers.setdefault(group, len(self.numbers))

    def block(self, rc, rx, ry):
        return (rc * self.X + rx) * self.Y + ry

    def dims(self, i):
        if i % 2 == 0:
            return "x", "y", self.X, self.Y
        return "y", "x", self.Y, self.X

    def place(self, axis, d):
        return (0, d, 0, 0) if axis == "x" else (0, 0, d, 0)

    def at_block(self, *pairs):
        steps = dict(zip(pairs[::2], pairs[1::2]))
        return self.block(0, steps.get("x", 0), steps.get("y", 0))

    def slot(self, axis, d):
        return d - 1 if axis == "x" else self.X - 2 + d

    def take(self, i):
        return self.w + LANES if i == self.n - 1 else self.w


def orders(p):
    X, Y, Z, R, T, n, w = p.X, p.Y, p.Z, p.R, p.tok, p.n, p.w
    tasks = {}

    def leave(it, i):
        out = [(("z", it, i, d), "z", T * p.take(i) * 2) for d in range(1, Z)]
        first, second, F, S = p.dims(i)
        for axis, count in ((first, F), (second, S)):
            out += [(("own", it, i, axis, d), axis, T * p.take(i) * 2) for d in range(1, count)]
        return out

    def core(it, i, b):
        return [(("blk", it, i, b + p.B), "c", R * p.take(i) * 2)]

    def add(name, deps=(), needs=(), sends=()):
        tasks[name] = (list(deps), list(needs), list(sends))

    def rest(it, i, axis, count):
        return [(("rest", it, i, axis, d), axis, (Z - 1) * T * p.take(i) * 2) for d in range(1, count)]

    for it in range(ITERS):
        for i in range(n):
            size = R * p.take(i) * 2
            first, second, F, S = p.dims(i)
            if it == 0:
                add(("enter", it, i), sends=leave(it, i))
                before = [("enter", it, i)]
            else:
                before = [("settle", it - 1, i)]
            add(("level1", it, i), before, [("z", it, i, d) for d in range(1, Z)],
                rest(it, i, first, F) + core(it, i, 0))
            after = [("level2", it, i - AHEAD, d) for d in range(1, p.dims(i - AHEAD)[2])] if i >= AHEAD else []
            add(("aside", it, i), [("level1", it, i)] + after, (), rest(it, i, second, S))
            for d in range(1, F):
                b = p.at_block(first, d)
                diag = [(("blk", it, i, p.at_block(first, d, second, g)), second, size) for g in range(1, S)]
                add(("level2", it, i, d), [("level1", it, i)],
                    [("own", it, i, first, d), ("rest", it, i, first, d)], diag + core(it, i, b))
                for g in range(1, S):
                    b = p.at_block(first, d, second, g)
                    add(("corner", it, i, d, g), [("level1", it, i)], [("blk", it, i, b)], core(it, i, b))
            for g in range(1, S):
                add(("level3", it, i, g), [("level1", it, i)],
                    [("own", it, i, second, g), ("rest", it, i, second, g)], core(it, i, p.at_block(second, g)))
            local = [t for t in tasks if t[0] in GATHER and t[1:3] == (it, i)]
            if i:
                local.append(("multiply", it, i - 1))
            add(("multiply", it, i), local, [("blk", it, i, b + p.B) for b in range(p.B)])
            add(("down", it, i), [("activate", it, 0)] + ([("down", it, i - 1)] if i else []), (),
                [(("core", it, i), "c", p.half * w * 2)])
            after = [("reduce2", it, i - BEHIND)] if i >= BEHIND else []
            add(("reduce1", it, i), [("down", it, i)] + after, [("core", it, i)],
                [(("first", it, i, a), first, S * R * w * 2) for a in range(1, F)])
            add(("reduce2", it, i), [("reduce1", it, i)], [("first", it, i, a) for a in range(1, F)],
                [(("second", it, i, b), second, R * w * 2) for b in range(1, S)])
            add(("reduce3", it, i), [("reduce2", it, i)], [("second", it, i, b) for b in range(1, S)],
                [(("back", it, i, d), "z", T * w * 2) for d in range(1, Z)])
            add(("settle", it, i), [("reduce3", it, i)] + ([("settle", it, i - 1)] if i else []),
                [("back", it, i, d) for d in range(1, Z)], leave(it + 1, i) if it + 1 < ITERS else [])
        for name, (deps, _, _) in tasks.items():
            if name[0] == "multiply" and name[1] == it:
                soon = range(name[2] + 1, name[2] + 1 + SOON)
                deps += [t for t in tasks if t[0] in GATHER and t[1] == it and t[2] in soon]
        add(("activate", it, 0), [("multiply", it, n - 1), ("weights", 0, 0)])
    add(("weights", 0, 0), [("enter", 0, n - 1)], [("route", r) for r in range(1, p.C * X)])

    p.bytes = 0
    for _, _, sends in tasks.values():
        for key, _, size in sends:
            p.lane(key)
            p.bytes += size
    p.lane(("route", 1))
    unit, table = 16 * p.U, (p.C * X - 1) * p.E * LANES * 4
    p.copies = next((m for m in range(1, 17) if (p.bytes + m * table) % unit == 0), 0)
    p.bytes += p.copies * table

    rate = {"x": LINK, "y": LINK, "z": LINK * 3 / Z, "c": 600.0e3}
    free = dict.fromkeys(rate, 0.0)
    arrival = {("route", r): 3.0 for r in range(1, p.C * X)}
    now, order, left = 0.0, [], dict(tasks)
    done = set()
    while left:
        best = None
        for position, (name, (deps, needs, _)) in enumerate(left.items()):
            if any(d not in done for d in deps) or any(k not in arrival for k in needs):
                continue
            ready = max([now] + [arrival[k] for k in needs])
            rank = (ready + (BONUS if name[0] in HEAVY else 0.0), RANK.get(name[0], 0), position)
            if best is None or rank < best[0]:
                best = (rank, name, ready)
        _, name, ready = best
        now = ready + COST[name[0]]
        for key, link, size in left[name][2]:
            begin = max(free[link], now)
            free[link] = begin + size / rate[link]
            arrival[key] = free[link] + LATENCY[link]
        done.add(name)
        order.append(name)
        del left[name]
    return order, now


def kernel(p, order, tokens_ref, gain_ref, ids_ref, weight_ref, gate_hbm, up_hbm, down_hbm, out_ref,
           wg, wu, wd, xg, z1, zn, asm, acc, hid, tab, tabs, wrow, state, keep, cs, cr,
           fs, fr, held, ss, sr, usum, own, bs, br, wsem, send_sem, recv_sem):
    C, X, Y, Z, R, w, T, n = p.C, p.X, p.Y, p.Z, p.R, p.w, p.tok, p.n
    e, h = lax.axis_index("expert"), lax.axis_index("hidden")
    x, c = e // C, e % C
    z, y = h // Y, h % Y

    def at(rc=0, rx=0, ry=0, rz=0):
        return ((x + rx) % X * C + (c + rc) % C, (z + rz) % Z * Y + (y + ry) % Y)

    loads = []
    for i in range(n):
        rows = pl.ds(i * w, w)
        loads.append(pltpu.make_async_copy(gate_hbm.at[0, rows, :], wg.at[rows, :], wsem.at[3 * i]))
        loads.append(pltpu.make_async_copy(up_hbm.at[0, rows, :], wu.at[rows, :], wsem.at[3 * i + 1]))
    for i in range(n):
        loads.append(pltpu.make_async_copy(down_hbm.at[0, :, pl.ds(i * w, w)], wd.at[i], wsem.at[3 * i + 2]))

    barrier = pltpu.get_barrier_semaphore()
    partners = [at(rc=rc, rx=rx) for rc in range(C) for rx in range(X) if rc or rx]
    partners += [at(ry=d) for d in range(1, Y)] + [at(rz=d) for d in range(1, Z)]
    for partner in partners:
        pl.semaphore_signal(barrier, inc=1, device_id=partner, device_id_type=MESH)
    for load in loads:
        load.start()

    def copy(key, src, dst, to):
        return pltpu.make_async_remote_copy(
            src_ref=src, dst_ref=dst, send_sem=send_sem.at[0], recv_sem=recv_sem.at[p.lane(key)],
            device_id=to, device_id_type=MESH)

    def send(*args):
        copy(*args).start()

    def arrived(key, dst):
        copy(key, dst, dst, at(rc=1)).wait_recv()

    def scales(square):
        scale = lax.rsqrt(square / p.D + EPSILON)
        high = scale.astype(bf16).astype(f32)
        middle = (scale - high).astype(bf16).astype(f32)
        low = scale - high - middle
        lane = lax.broadcasted_iota(jnp.int32, (T, LANES), 1)
        parts = jnp.where(lane == 0, high, jnp.where(lane == 1, middle, jnp.where(lane == 2, low, 0.0)))
        return parts.astype(bf16)

    squares = [None] * ITERS

    def prepare(it, i, values):
        cols = pl.ds(i * w, w)
        square = jnp.sum(values * values, axis=-1, keepdims=True)
        squares[it] = square if i == 0 else squares[it] + square
        z1[it, i, 0, :, 0:w] = (values * gain_ref[:, cols]).astype(bf16)
        if i == n - 1:
            z1[it, i, 0, :, w:w + LANES] = scales(squares[it])

    def around(axis, d):
        return at(rx=d) if axis == "x" else at(ry=d)

    def back_from(axis, d):
        return ((X if axis == "x" else Y) - d) % (X if axis == "x" else Y)

    def slab(it, i, d):
        return z1.at[it, i, d, :, pl.ds(0, p.take(i))]

    def near(it, i, axis, d, part):
        full = zn.at[it, i, p.slot(axis, d)]
        return full.at[part, :, pl.ds(0, p.take(i))]

    def enter(it, i):
        for d in range(1, Z):
            send(("z", it, i, Z - d), slab(it, i, 0), slab(it, i, Z - d), at(rz=d))
        first, second, F, S = p.dims(i)
        for axis, count in ((first, F), (second, S)):
            for d in range(1, count):
                g = back_from(axis, d)
                send(("own", it, i, axis, g), slab(it, i, 0), near(it, i, axis, g, 0), around(axis, d))

    def rest(it, i, axis, count):
        for d in range(1, count):
            g = back_from(axis, d)
            send(("rest", it, i, axis, g), z1.at[it, i, pl.ds(1, Z - 1), :, pl.ds(0, p.take(i))],
                 near(it, i, axis, g, pl.ds(1, Z - 1)), around(axis, d))

    def gather_near(it, i, axis, d):
        arrived(("own", it, i, axis, d), near(it, i, axis, d, pl.ds(0, Z)))
        b = p.at_block(axis, d)
        join(it, i, b, lambda k, wide: zn[it, i, p.slot(axis, d), k, :, 0:wide])
        return b

    def join(it, i, b, part):
        wide = p.take(i)
        for d in range(Z):
            asm[d * T:(d + 1) * T, 0:wide] = part(d, wide).astype(f32)
        xg[it, i, b, :, 0:wide] = asm[:, 0:wide].astype(bf16)

    values = tokens_ref[...].astype(f32)
    state[...] = values
    for i in range(n):
        prepare(0, i, values[:, i * w:(i + 1) * w])
    L = p.H * T
    which = lax.broadcasted_iota(jnp.int32, (p.E, L), 0)
    tab[...] = jnp.zeros_like(tab)
    tab[0, :, 0:L] = (jnp.where(ids_ref[0:1, :] == which, weight_ref[0:1, :], 0.0)
                   + jnp.where(ids_ref[1:2, :] == which, weight_ref[1:2, :], 0.0))
    pl.semaphore_wait(barrier, len(partners))

    def weights(*_):
        lane = lax.broadcasted_iota(jnp.int32, (T, LANES), 1)
        token = lax.broadcasted_iota(jnp.int32, (T, LANES), 0)
        expert = lax.broadcasted_iota(jnp.int32, (p.E, LANES), 0)
        arrived(("route", 1), tabs.at[pl.ds(1, C * X - 1)])
        for rc in range(C):
            for rx in range(X):
                r = rc * X + rx
                table = tabs[r, 0] if r else tab[0]
                mine = jnp.sum(jnp.where(expert == e, table, 0.0), axis=0, keepdims=True)
                for ry in range(Y):
                    for rz in range(Z):
                        _, whose = at(ry=ry, rz=rz)
                        part = jnp.where(lane == whose * T + token, mine, 0.0)
                        base = p.block(rc, rx, ry) * R + rz * T
                        wrow[base:base + T, :] = jnp.broadcast_to(
                            jnp.sum(part, axis=1, keepdims=True), (T, LANES))

    def piece(it, i, b):
        return xg.at[it, i, b, :, pl.ds(0, p.take(i))]

    def block_to(it, i, b_from, rc, rx, ry):
        b, rest = b_from % Y, b_from // Y
        fx, fc = rest % X, rest // X
        there = p.block((fc - rc) % C, (fx - rx) % X, (b - ry) % Y)
        send(("blk", it, i, there), piece(it, i, b_from), piece(it, i, there), at(rc, rx, ry))

    def got(it, i, b, count=1):
        arrived(("blk", it, i, b), piece(it, i, pl.ds(b, count)))

    def level1(it, i):
        arrived(("z", it, i, 1), slab(it, i, pl.ds(1, Z - 1)))
        first, _, F, _ = p.dims(i)
        rest(it, i, first, F)
        join(it, i, 0, lambda k, wide: z1[it, i, k, :, 0:wide])
        block_to(it, i, 0, 1, 0, 0)

    def aside(it, i):
        _, second, _, S = p.dims(i)
        rest(it, i, second, S)

    def level2(it, i, d):
        first, second, _, S = p.dims(i)
        b = gather_near(it, i, first, d)
        for g in range(1, S):
            block_to(it, i, b, *p.place(second, g)[:3])
        block_to(it, i, b, 1, 0, 0)

    def level3(it, i, g):
        b = gather_near(it, i, p.dims(i)[1], g)
        block_to(it, i, b, 1, 0, 0)

    def corner(it, i, d, g):
        first, second, _, _ = p.dims(i)
        b = p.at_block(first, d, second, g)
        got(it, i, b)
        block_to(it, i, b, 1, 0, 0)

    def multiply(it, i):
        got(it, i, p.B, p.B)
        if it == 0:
            loads[2 * i].wait()
            loads[2 * i + 1].wait()
        block = xg[it, i, :, :, 0:w].reshape(p.rows, w)
        for side, weight in ((0, wg), (1, wu)):
            product = jnp.dot(block, weight[i * w:(i + 1) * w, :], preferred_element_type=f32)
            if i == 0:
                acc[side] = product
            else:
                acc[side] += product

    def activate(it, _):
        parts = xg[it, n - 1, :, :, w:w + LANES].reshape(p.rows, LANES).astype(f32)
        scale = jnp.broadcast_to(jnp.sum(parts, axis=1, keepdims=True), (p.rows, LANES))
        mine = wrow[...]
        for k in range(p.U // LANES):
            cols = slice(k * LANES, (k + 1) * LANES)
            gate = acc[0, :, cols] * scale
            units = gate / (1.0 + jnp.exp(-gate)) * (acc[1, :, cols] * scale)
            hid[:, cols] = (units * mine).astype(bf16)

    def down(it, i):
        if it == 0:
            loads[2 * n + i].wait()
        product = jnp.dot(hid[...], wd[i], preferred_element_type=f32)
        cs[it, i] = product[p.half:, :].astype(bf16)
        send(("core", it, i), cs.at[it, i], cr.at[it, i], at(rc=1))
        keep[i] = product[:p.half, :]

    def reduce1(it, i):
        arrived(("core", it, i), cr.at[it, i])
        first, _, F, S = p.dims(i)
        for a in list(range(1, F)) + [0]:
            for b in range(S):
                b_at = p.block(0, a, b) if first == "x" else p.block(0, b, a)
                rows = pl.ds(b_at * R, R)
                total = keep[i, rows, :] + cr[it, i, rows, :].astype(f32)
                if a:
                    fs[it, i, (a - 1) * S + b] = total.astype(bf16)
                else:
                    held[i, b] = total
            if a:
                send(("first", it, i, a), fs.at[it, i, pl.ds((a - 1) * S, S)],
                     fr.at[it, i, pl.ds((a - 1) * S, S)], at(*p.place(first, a)[:3]))

    def reduce2(it, i):
        _, second, F, S = p.dims(i)
        for a in range(1, F):
            arrived(("first", it, i, a), fr.at[it, i, pl.ds((a - 1) * S, S)])
        for b in list(range(1, S)) + [0]:
            total = held[i, b]
            for a in range(1, F):
                total = total + fr[it, i, (a - 1) * S + b].astype(f32)
            if b:
                ss[it, i, b - 1] = total.astype(bf16)
                send(("second", it, i, b), ss.at[it, i, b - 1], sr.at[it, i, b - 1], at(*p.place(second, b)[:3]))
            else:
                usum[i] = total

    def reduce3(it, i):
        S = p.dims(i)[3]
        total = usum[i]
        for b in range(1, S):
            arrived(("second", it, i, b), sr.at[it, i, b - 1])
            total = total + sr[it, i, b - 1].astype(f32)
        asm[:, 0:w] = total
        for d in range(1, Z):
            bs[it, i, d - 1] = asm[d * T:(d + 1) * T, 0:w].astype(bf16)
            send(("back", it, i, d), bs.at[it, i, d - 1], br.at[it, i, d - 1], at(rz=d))
        own[i] = asm[0:T, 0:w]

    def settle(it, i):
        mixed = own[i]
        arrived(("back", it, i, 1), br.at[it, i])
        for d in range(1, Z):
            mixed = mixed + br[it, i, d - 1].astype(f32)
        cols = pl.ds(i * w, w)
        fresh = (NUDGE * state[:, cols] + NUDGE * (tokens_ref[:, cols].astype(f32) + mixed)).astype(bf16)
        if it + 1 < ITERS:
            state[:, cols] = fresh.astype(f32)
            prepare(it + 1, i, fresh.astype(f32))
            enter(it + 1, i)
        else:
            out_ref[:, cols] = fresh

    steps = dict(enter=enter, level1=level1, aside=aside, level2=level2, level3=level3, corner=corner, multiply=multiply, activate=activate,
                 down=down, reduce1=reduce1, reduce2=reduce2, reduce3=reduce3, settle=settle, weights=weights)
    for name in order:
        steps[name[0]](*name[1:])
        if name == ("enter", 0, 0):
            for rc in range(C):
                for rx in range(X):
                    if rc or rx:
                        r = ((-rc) % C) * X + (-rx) % X
                        send(("route", r), tab, tabs.at[r], at(rc=rc, rx=rx))
    whole = wg.at[pl.ds(0, p.bytes // (2 * p.U)), :]
    pltpu.make_async_copy(whole, whole, send_sem.at[0]).wait()


def deep_scratch(p):
    X, Y, Z, R, w, T, n, U = p.X, p.Y, p.Z, p.R, p.w, p.tok, p.n, p.U
    S, FS = max(X, Y), max((X - 1) * Y, (Y - 1) * X)
    wide, rows, half = w + LANES, p.rows, p.half
    return [
        ((p.D, U), bf16), ((p.D, U), bf16), ((n, U, w), bf16),
        ((ITERS, n, p.NB, R, wide), bf16),
        ((ITERS, n, Z, T, wide), bf16), ((ITERS, n, X + Y - 2, Z, T, wide), bf16), ((R, wide), f32),
        ((2, rows, U), f32), ((rows, U), bf16),
        ((p.copies, p.E, LANES), f32), ((p.E, p.copies, p.E, LANES), f32), ((rows, LANES), f32),
        ((T, p.D), f32),
        ((n, half, w), f32), ((ITERS, n, half, w), bf16), ((ITERS, n, half, w), bf16),
        ((ITERS, n, FS, R, w), bf16), ((ITERS, n, FS, R, w), bf16),
        ((n, S, R, w), f32),
        ((ITERS, n, S - 1, R, w), bf16), ((ITERS, n, S - 1, R, w), bf16),
        ((n, R, w), f32),
        ((n, T, w), f32),
        ((ITERS, n, Z - 1, T, w), bf16), ((ITERS, n, Z - 1, T, w), bf16),
    ]


def on_device(experts, hidden, tokens, norm_gain, gate_weight, up_weight, down_weight, expert_ids, route_weight):
    tok, width = tokens.shape
    p = Deep(experts, hidden, tok, width, gate_weight.shape[2])
    order, _ = orders(p)
    buffers = deep_scratch(p)
    size = sum(math.prod(shape) * (4 if kind == f32 else 2) for shape, kind in buffers)
    if size > VMEM_BYTES * 9 // 10 or hidden * tok > LANES:
        return on_device_compact(experts, hidden, tokens, norm_gain, gate_weight, up_weight, down_weight,
                                 expert_ids, route_weight)
    if not p.copies or p.bytes > 2 * p.U * width:
        raise ValueError("send total")
    count = len(p.numbers)
    dma = pltpu.SemaphoreType.DMA
    inside = pl.BlockSpec(memory_space=pltpu.VMEM)
    outside = pl.BlockSpec(memory_space=pl.ANY)
    return pl.pallas_call(
        functools.partial(kernel, p, order),
        out_shape=jax.ShapeDtypeStruct((tok, width), bf16),
        in_specs=[inside] * 4 + [outside] * 3,
        out_specs=inside,
        scratch_shapes=[pltpu.VMEM(*b) for b in buffers] + [dma((3 * p.n,)), dma((1,)), dma((count,))],
        compiler_params=pltpu.CompilerParams(
            collective_id=0, has_side_effects=True, vmem_limit_bytes=VMEM_BYTES),
        name="settle",
    )(tokens, norm_gain.reshape(1, width), expert_ids.T, route_weight.T, gate_weight, up_weight, down_weight)


def solution(mesh):
    placed = (
        P(("expert", "hidden"), None),
        P(),
        P("expert", None, "hidden"),
        P("expert", None, "hidden"),
        P("expert", "hidden", None),
        P("expert", None),
        P("expert", None),
    )
    return jax.shard_map(
        functools.partial(on_device, mesh.shape["expert"], mesh.shape["hidden"]),
        mesh=mesh,
        in_specs=placed,
        out_specs=P(("expert", "hidden"), None),
        check_vma=False,
    )
```
